32 devices in a mesh: groups: 2 (over y), cls: 4 (over z), img: 4 (over x, core).
Axes of the slice: x: 2, y: 2, z: 4, core: 2. Of those that a mesh axis runs over, the one named last changes fastest.
Arguments:
- particles: bfloat16 [512, 2, 4608], P(('groups', 'img', 'cls')), parts along dimension 0, may hold values from -30 to 30
- classes: bfloat16 [256, 2, 4608], P(('groups', 'cls')), parts along dimension 0, may hold values from -4 to 4
- ctf: float32 [128, 4608], P('groups'), parts along dimension 0, may hold values from 0.1 to 1
- noise_weight: float32 [9216], P('groups'), parts along dimension 0, may hold values from 0.01 to 0.1
- group_ids: int32 [512], P(('groups', 'img', 'cls')), parts along dimension 0, may hold values from 0 to 63
- shifts: int32 [48, 2], P('groups'), parts along dimension 0, may hold values from -6 to 6
Outputs:
- log_resp: float32 [512, 128], P(('groups', 'img'), 'cls'), parts along dimension 0
- averages: float32 [256, 2, 4608], P(('groups', 'cls'), None, 'img'), parts along dimension 0
The draws below stay inside these ranges and needn't reach their ends.
There are 2 independent parts, one for each index of `groups`. The reference program is written for one: setup_inputs(seed, part) draws one part's arguments, and reference() takes and returns one part's arrays. A program takes and returns all parts, laid end to end along the dimension named above; each array names one. Nothing has to cross between parts.
All inputs are finite; a program needn't handle non-finite values.
Results may differ from the reference program's by a relative error of at most 0.012.
The reference program's roundings to bfloat16 on the way (of `templates`, `weighted` and `rho_low`) count: a program that leaves them out, or rounds other values in their place, can miss the bound.
Values may be sent and summed in bfloat16 or wider, within the bound.
A program may use at most 128 MiB of HBM per device.

```python
import math
import jax
import jax.numpy as jnp
from jax import lax

FREQ = 4608
BOX = 128
POSES = 24
GROUPS = 64
CLASSES = 128
PARTICLES = 256


def class_values(key):
    inner = jax.random.fold_in(key, 11)
    values = jnp.clip(jax.random.normal(inner, (CLASSES, 2, FREQ), jnp.float32), -4.0, 4.0)
    return values


def draw_classes(key, part):
    return class_values(key).astype(jnp.bfloat16)


def draw_shifts(key, part):
    return jax.random.randint(jax.random.fold_in(key, 12), (POSES, 2), -6, 7).astype(jnp.int32)


def rotate_rows(values, cos_rows, sin_rows):
    real_part = values[:, 0, :]
    imag_part = values[:, 1, :]
    return jnp.stack([real_part * cos_rows - imag_part * sin_rows, real_part * sin_rows + imag_part * cos_rows], axis=1)


def draw_particles(key, part):
    key_noise = jax.random.fold_in(key, 21)
    key_class = jax.random.fold_in(key, 23)
    key_pose = jax.random.fold_in(key, 24)
    noise = jnp.clip(jax.random.normal(key_noise, (PARTICLES, 2, FREQ), jnp.float32), -4.0, 4.0)
    values = class_values(key).astype(jnp.bfloat16).astype(jnp.float32)
    shifts = draw_shifts(key, part)
    first = jax.random.randint(key_class, (PARTICLES,), 0, CLASSES)
    second = (first + 1) % CLASSES
    pose = jax.random.randint(key_pose, (PARTICLES,), 0, POSES)
    index = jnp.arange(FREQ)
    along_y = (index // BOX).astype(jnp.float32)
    along_x = (index % BOX - BOX // 2).astype(jnp.float32)
    chosen = shifts[pose]
    angle = 2.0 * jnp.pi / BOX * (chosen[:, 0:1].astype(jnp.float32) * along_x[None, :] + chosen[:, 1:2].astype(jnp.float32) * along_y[None, :])
    cos_rows = jnp.cos(angle)
    sin_rows = jnp.sin(angle)
    planted = rotate_rows(values[first], cos_rows, sin_rows) + 0.992 * rotate_rows(values[second], cos_rows, sin_rows)
    rows = jnp.arange(PARTICLES)
    boost = 4608.0 / FREQ
    strength = boost * jnp.where(rows % 3 == 0, 0.9, jnp.where(rows % 3 == 1, 1.3, 1.8))
    chosen_rows = rows % 61 == 7
    result = jnp.where(chosen_rows[:, None, None], strength[:, None, None] * planted, noise)
    return result.astype(jnp.bfloat16)


def with_ends(values, own_key, smallest, top_value):
    extent = values.shape
    index_at = [jax.random.randint(jax.random.fold_in(own_key, axis), (), 0, extent[axis]) for axis in range(len(extent))]
    values = values.at[tuple(index_at)].set(smallest)
    longest = extent.index(max(extent))
    index_at[longest] = (index_at[longest] + 1) % extent[longest]
    return values.at[tuple(index_at)].set(top_value)


def setup_inputs(seed: int = 0, part: int = 0) -> dict:
    splits = jax.random.split(jax.random.key(seed), 7)
    part_splits = jax.random.split(jax.random.fold_in(splits[6], part), 7)
    particles = draw_particles(jax.random.fold_in(jax.random.fold_in(splits[6], part), 71), part)
    classes = draw_classes(jax.random.fold_in(jax.random.fold_in(splits[6], part), 71), part)
    ctf = jnp.clip(jax.random.uniform(part_splits[2], (GROUPS, FREQ), jnp.float32, 0.1, 1.0), 0.1, 1.0)
    noise_weight = jnp.clip(jnp.exp(jax.random.uniform(part_splits[3], (FREQ,), jnp.float32, math.log(0.01), math.log(0.1))), 0.01, 0.1)
    group_ids = with_ends(jax.random.randint(part_splits[4], (PARTICLES,), 0, GROUPS), jax.random.fold_in(part_splits[4], 1), 0, GROUPS - 1).astype(jnp.int32)
    shifts = draw_shifts(jax.random.fold_in(jax.random.fold_in(splits[6], part), 71), part)
    return dict(particles=particles, classes=classes, ctf=ctf, noise_weight=noise_weight, group_ids=group_ids, shifts=shifts)


prior_precision = 0.02


def phase_tables(shifts):
    index = jnp.arange(FREQ)
    along_y = (index // BOX).astype(jnp.float32)
    along_x = (index % BOX - BOX // 2).astype(jnp.float32)
    angle = (2.0 * jnp.pi / BOX) * (shifts[:, 0:1].astype(jnp.float32) * along_x[None, :] + shifts[:, 1:2].astype(jnp.float32) * along_y[None, :])
    return jnp.cos(angle), jnp.sin(angle)


def reference(particles, classes, ctf, noise_weight, group_ids, shifts):
    cos_t, sin_t = phase_tables(shifts)
    real_part = classes[:, 0, :].astype(jnp.float32)
    imag_part = classes[:, 1, :].astype(jnp.float32)
    temp_re = real_part[None] * cos_t[:, None, :] - imag_part[None] * sin_t[:, None, :]
    temp_im = real_part[None] * sin_t[:, None, :] + imag_part[None] * cos_t[:, None, :]
    templates = jnp.stack([temp_re, temp_im], axis=2).astype(jnp.bfloat16)
    templates = templates.reshape(POSES * CLASSES, 2 * FREQ)
    selected = ctf[group_ids]
    weighted = (particles.astype(jnp.float32) * (selected * noise_weight[None, :])[:, None, :]).astype(jnp.bfloat16)
    weighted = weighted.reshape(PARTICLES, 2 * FREQ)
    ctf_weight = ctf * ctf * noise_weight[None, :]
    power = jnp.dot(ctf_weight, (real_part * real_part + imag_part * imag_part).T, precision=lax.Precision.HIGHEST)
    penalty = power[group_ids]
    cross = jnp.dot(weighted.astype(jnp.float32), templates.astype(jnp.float32).T, precision=lax.Precision.HIGHEST)
    scores = cross.reshape(PARTICLES, POSES, CLASSES) - 0.5 * penalty[:, None, :]
    peak = jnp.max(scores, axis=(1, 2))
    log_norm = peak + jnp.log(jnp.sum(jnp.exp(scores - peak[:, None, None]), axis=(1, 2)))
    pose_peak = jnp.max(scores, axis=1)
    log_resp = pose_peak + jnp.log(jnp.sum(jnp.exp(scores - pose_peak[:, None, :]), axis=1)) - log_norm[:, None]
    rho = jnp.exp(scores - log_norm[:, None, None])
    rho_low = rho.astype(jnp.bfloat16).reshape(PARTICLES, POSES * CLASSES)
    sums = jnp.dot(rho_low.astype(jnp.float32).T, weighted.astype(jnp.float32), precision=lax.Precision.HIGHEST)
    sums = sums.reshape(POSES, CLASSES, 2, FREQ)
    cos_b = cos_t[:, None, :]
    sin_b = sin_t[:, None, :]
    numer_re = jnp.sum(sums[:, :, 0, :] * cos_b + sums[:, :, 1, :] * sin_b, axis=0)
    numer_im = jnp.sum(sums[:, :, 1, :] * cos_b - sums[:, :, 0, :] * sin_b, axis=0)
    numer = jnp.stack([numer_re, numer_im], axis=1)
    onehot = (group_ids[:, None] == jnp.arange(GROUPS)[None, :]).astype(jnp.float32)
    pose_total = jnp.sum(rho, axis=1)
    mass = jnp.dot(pose_total.T, onehot, precision=lax.Precision.HIGHEST)
    denom = jnp.dot(mass, ctf_weight, precision=lax.Precision.HIGHEST)
    averages = numer / (denom[:, None, :] + prior_precision)
    return log_resp, averages
```

```python
import functools

import jax
import jax.numpy as jnp
from jax import lax
from jax.experimental import pallas as pl
from jax.experimental.pallas import tpu as pltpu
from jax.sharding import PartitionSpec as P

BOX = 128
LANES = 128
MESH = pl.DeviceIdType.MESH
HIGHEST = lax.Precision.HIGHEST
NT = (((1,), (1,)), ((), ()))
F32 = jnp.float32
BF16 = jnp.bfloat16

prior_precision = 0.02


def fill_phase_tables(shift_ref, cos_ref, sin_ref):
    poses, freq = cos_ref.shape
    step = 2.0 * jnp.pi / BOX
    lane = lax.broadcasted_iota(jnp.int32, (poses, BOX), 1)
    pose = lax.broadcasted_iota(jnp.int32, (poses, BOX), 0)
    move_x = jnp.zeros((poses, BOX), jnp.int32)
    move_y = jnp.zeros((poses, BOX), jnp.int32)
    for r in range(poses):
        move_x = jnp.where(pose == r, shift_ref[0, r], move_x)
        move_y = jnp.where(pose == r, shift_ref[1, r], move_y)
    move_x, move_y = move_x.astype(jnp.float32), move_y.astype(jnp.float32)
    angle_x = step * (move_x * (lane - BOX // 2).astype(jnp.float32))
    cos_x, sin_x = jnp.cos(angle_x), jnp.sin(angle_x)
    for row in range(freq // BOX):
        if row % BOX == 0:
            angle_y = step * (move_y * (lane + row).astype(jnp.float32))
            cos_rows, sin_rows = jnp.cos(angle_y), jnp.sin(angle_y)
        cos_y = cos_rows[:, row % BOX : row % BOX + 1]
        sin_y = sin_rows[:, row % BOX : row % BOX + 1]
        cols = slice(row * BOX, (row + 1) * BOX)
        cos_ref[:, cols] = cos_x * cos_y - sin_x * sin_y
        sin_ref[:, cols] = sin_x * cos_y + cos_x * sin_y


def kernel(
    n_cls, n_img, near, cores, chunk,
    ids_s, shift_ref, part_hbm, cls_hbm, ctf_hbm, nw_hbm,
    resp_ref, avg_ref,
    part_ref, cls_raw, ctf_ref, nw_ref, sel, onehot, marks, wide_marks, cos_ref, sin_ref,
    wbuf, turned, cls_mat, power_buf, scores, rho_low, stat, resp_send, resp_recv,
    mass_part, mass_recv, mass_all,
    core_send, core_recv, row_send, row_recv, far_send, far_recv, own,
    in_sem, cq_s, cq_r, cf_s, cf_r, wh_s, wh_r, mk_s, mk_r, pw_s, pw_r, st_s, st_r, rp_s, rp_r,
    m1_s, m1_r, m2_s, m2_r, c1_s, c1_r, r2_s, r2_r, o2_s, o2_r, f3_s, f3_r,
):
    rows = part_ref.shape[0]
    freq = ctf_ref.shape[1]
    groups = ctf_ref.shape[0]
    classes = cls_raw.shape[1]
    poses = cos_ref.shape[0]
    far = n_cls // near
    outer = n_img // cores
    part_freq = freq // n_img
    steps = part_freq // chunk
    wide = 2 * chunk
    block = poses * rows
    held = far * classes
    my_cls = lax.axis_index("cls")
    my_img = lax.axis_index("img")
    q, h = my_cls // near, lax.rem(my_cls, near)
    u, v = my_img // cores, lax.rem(my_img, cores)

    def near_id(d):
        return {"cls": q * near + lax.rem(h + d, near)}

    def far_id(d):
        return {"cls": lax.rem(q + d, far) * near + h}

    def img_id(d):
        return {"img": lax.rem(my_img + d, n_img)}

    def core_id(d):
        return {"img": u * cores + lax.rem(v + d, cores)}

    def outer_id(d):
        return {"img": lax.rem(u + d, outer) * cores + v}

    def remote(src, dst, send, recv, device):
        return pltpu.make_async_remote_copy(
            src_ref=src, dst_ref=dst, send_sem=send, recv_sem=recv,
            device_id=device, device_id_type=MESH,
        )

    barrier = pltpu.get_barrier_semaphore()
    peers = (
        [near_id(d) for d in range(1, near)]
        + [far_id(d) for d in range(1, far)]
        + [img_id(d) for d in range(1, n_img)]
    )
    for peer in peers:
        pl.semaphore_signal(barrier, inc=1, device_id=peer, device_id_type=MESH)

    inputs = [
        pltpu.make_async_copy(src, dst, in_sem.at[i])
        for i, (src, dst) in enumerate(
            ((ctf_hbm, ctf_ref), (nw_hbm, nw_ref.at[0]), (part_hbm, part_ref), (cls_hbm, cls_raw.at[0]))
        )
    ]
    for copy in inputs:
        copy.start()

    def freq_at(img, p):
        return pl.multiple_of(img * part_freq + p * chunk, LANES)

    def cls_far(d, p):
        cols = pl.ds(freq_at(my_img, p), chunk)
        return remote(
            cls_hbm.at[:, :, cols], cls_raw.at[far - d, :, :, cols],
            cq_s.at[d, p], cq_r.at[d, p], far_id(d),
        )

    def cls_forward(j, p, e, img):
        cols = pl.ds(freq_at(img, p), chunk)
        piece = cls_raw.at[j, :, :, cols]
        return remote(piece, piece, cf_s.at[j, p, e], cf_r.at[j, p, e], img_id(e))

    def w_near(d, p):
        return remote(
            wbuf.at[p, 0], wbuf.at[p, near - d], wh_s.at[d, p], wh_r.at[d, p], near_id(d)
        )

    def marks_near(d):
        return remote(marks.at[0], marks.at[near - d], mk_s.at[d], mk_r.at[d], near_id(d))

    def power_far(d):
        return remote(
            power_buf.at[0], power_buf.at[far - d], pw_s.at[d], pw_r.at[d], far_id(d)
        )

    pl.semaphore_wait(barrier, len(peers))
    for p in range(steps):
        for d in range(1, far):
            cls_far(d, p).start()

    for copy in inputs[:3]:
        copy.wait()
    for i in range(rows):
        sel[pl.ds(i, 1), :] = ctf_ref[pl.ds(ids_s[i], 1), :] * nw_ref[...]
        onehot[pl.ds(i, 1), :] = (
            lax.broadcasted_iota(jnp.int32, (1, onehot.shape[1]), 1) == ids_s[i]
        ).astype(F32)
    for p in range(steps):
        for i in range(n_img):
            cols = slice(i * part_freq + p * chunk, i * part_freq + (p + 1) * chunk)
            for part in range(2):
                at = i * wide + part * chunk
                wbuf[p, 0, :, at : at + chunk] = (
                    part_ref[:, part, cols].astype(F32) * sel[:, cols]
                ).astype(BF16)
        for d in range(1, near):
            w_near(d, p).start()
    marks[0] = onehot[...].astype(BF16)
    for d in range(1, near):
        marks_near(d).start()

    fill_phase_tables(shift_ref, cos_ref, sin_ref)

    def turn(p, b):
        def one(i, carry):
            at = pl.ds(freq_at(i, p), chunk)
            re_at = pl.ds(pl.multiple_of(i * wide, LANES), chunk)
            im_at = pl.ds(pl.multiple_of(i * wide + chunk, LANES), chunk)
            re = wbuf[p, b, :, re_at].astype(F32)
            im = wbuf[p, b, :, im_at].astype(F32)
            for r in range(poses):
                cos_r = cos_ref[r : r + 1, at]
                sin_r = sin_ref[r : r + 1, at]
                out = slice(b * block + r * rows, b * block + (r + 1) * rows)
                turned[p, out, re_at] = (re * cos_r + im * sin_r).astype(BF16)
                turned[p, out, im_at] = (im * cos_r - re * sin_r).astype(BF16)
            return carry

        lax.fori_loop(0, n_img, one, 0)

    def relay(p):
        for d in range(1, far):
            cls_far(d, p).wait_recv()
            for e in [*range(cores, n_img), *range(1, cores)]:
                cls_forward(far - d, p, e, my_img).start()

    def turn_own(p, carry):
        turn(p, 0)
        return carry

    lax.fori_loop(0, 1, turn_own, 0)
    inputs[3].wait()
    relay(0)
    lax.fori_loop(1, steps, turn_own, 0)

    def power_step(c, total):
        at = pl.ds(pl.multiple_of(c * chunk, LANES), chunk)
        re = cls_raw[0, :, 0, at].astype(F32)
        im = cls_raw[0, :, 1, at].astype(F32)
        ctf = ctf_ref[:, at]
        return total + lax.dot_general(
            re * re + im * im, ctf * ctf * nw_ref[:, at], NT, precision=HIGHEST,
            preferred_element_type=F32,
        )

    power = lax.fori_loop(0, freq // chunk, power_step, jnp.zeros((classes, groups), F32))
    power_buf[0] = jnp.zeros_like(power_buf[0])
    power_buf[0, :, :groups] = power
    for d in range(1, far):
        power_far(d).start()
    if steps > 1:
        relay(1)

    for d in range(1, near):
        marks_near(d).wait_recv()
    for b in range(near):
        for r in range(poses):
            wide_marks[b * block + r * rows : b * block + (r + 1) * rows, :] = marks[b]
    for d in range(1, far):
        power_far(d).wait_recv()
    rest = -0.5 * power_buf[...].reshape(held, power_buf.shape[2])
    penalty = jnp.zeros(scores.shape, F32)
    for _ in range(3):
        top = rest.astype(BF16)
        rest = rest - top.astype(F32)
        penalty += lax.dot_general(top, wide_marks[...], NT, preferred_element_type=F32)
    scores[...] = penalty

    def match(p):
        for j in range(1, far):
            for e in range(1, n_img):
                cls_forward(j, p, e, lax.rem(my_img + n_img - e, n_img)).wait_recv()

        def lay(i, carry):
            at = pl.ds(freq_at(i, p), chunk)
            for j in range(far):
                for part in range(2):
                    cls_mat[
                        j * classes : (j + 1) * classes,
                        pl.ds(pl.multiple_of(i * wide + part * chunk, LANES), chunk),
                    ] = cls_raw[j, :, part, at]
            return carry

        lax.fori_loop(0, n_img, lay, 0)
        for d in range(1, near):
            w_near(d, p).wait_recv()
            turn(p, near - d)
        scores[...] += lax.dot_general(
            cls_mat[...], turned[p], NT, preferred_element_type=F32
        )

    for p in range(steps):
        match(p)
        if p + 2 < steps:
            relay(p + 2)

    tiles = block // LANES

    def over_poses(op, pieces):
        value = functools.reduce(op, pieces)
        shift = LANES // 2
        while shift >= rows:
            value = op(value, pltpu.roll(value, shift, 1))
            shift //= 2
        return value

    def tile(b, t):
        return slice(b * block + t * LANES, b * block + (t + 1) * LANES)

    pose_peak, pose_sum, peak, mass_sum = [], [], [], []
    for b in range(near):
        top = over_poses(jnp.maximum, [scores[:, tile(b, t)] for t in range(tiles)])
        total = over_poses(jnp.add, [jnp.exp(scores[:, tile(b, t)] - top) for t in range(tiles)])
        whole = jnp.max(top, axis=0, keepdims=True)
        pose_peak.append(top)
        pose_sum.append(total)
        peak.append(whole)
        mass_sum.append(jnp.sum(total * jnp.exp(top - whole), axis=0, keepdims=True))
        stat[0, b : b + 1, :] = whole
        stat[0, near + b : near + b + 1, :] = mass_sum[b]

    def stat_near(d):
        return remote(stat.at[0], stat.at[d], st_s.at[d], st_r.at[d], near_id(d))

    for d in range(1, near):
        stat_near(d).start()
    log_sums = [pose_peak[b] + jnp.log(pose_sum[b]) for b in range(near)]
    for d in range(1, near):
        stat_near(d).wait_recv()
    mass = jnp.zeros((held, marks.shape[2]), F32)
    lane = lax.broadcasted_iota(jnp.int32, (1, LANES), 1)
    lane_h = lax.rem(lane // rows, near)
    both = jnp.zeros((held, LANES), F32)
    for b in range(near):
        tops = [stat[d, (b + d) % near : (b + d) % near + 1, :] for d in range(near)]
        sums = [stat[d, near + (b + d) % near : near + (b + d) % near + 1, :] for d in range(near)]
        whole = functools.reduce(jnp.maximum, tops)
        norm = functools.reduce(jnp.add, [s * jnp.exp(t - whole) for s, t in zip(sums, tops)])
        log_norm = whole + jnp.log(norm)
        for t in range(tiles):
            rho_low[:, tile(b, t)] = jnp.exp(scores[:, tile(b, t)] - log_norm).astype(BF16)
        pose_total = pose_sum[b] * jnp.exp(pose_peak[b] - log_norm)
        mass_sum[b] = jnp.where(lane < rows, pose_total, 0.0)
        both = jnp.where(lane_h == lax.rem(h + b, near), log_sums[b] - log_norm, both)
    resp_send[...] = both.reshape(resp_send.shape)

    def resp_far(d):
        return remote(resp_send.at[d], resp_recv.at[far - d], rp_s.at[d], rp_r.at[d], far_id(d))

    for d in range(1, far):
        resp_far(d).start()

    def numer(img, p):
        return jnp.dot(
            rho_low[...], turned[p, :, pl.ds(pl.multiple_of(img * wide, LANES), wide)],
            preferred_element_type=F32,
        )

    def slice_of(du, dv):
        return lax.rem(u + du, outer) * cores + lax.rem(v + dv, cores)

    def core_copy(du, dv, p):
        return remote(
            core_send.at[du, dv - 1, p], core_recv.at[du, dv - 1, p],
            c1_s.at[du, dv, p], c1_r.at[du, dv, p], core_id(dv),
        )

    def row_copy(du, p, theirs):
        part = pl.ds(classes, held - classes) if theirs else pl.ds(0, classes)
        send, recv = (r2_s, r2_r) if theirs else (o2_s, o2_r)
        return remote(
            row_send.at[du - 1, p, part], row_recv.at[du - 1, p, part],
            send.at[du, p], recv.at[du, p], outer_id(du),
        )

    def mass_far(d):
        return remote(
            mass_part.at[d], mass_recv.at[d], m1_s.at[d], m1_r.at[d], far_id(d)
        )

    def mass_img(d):
        return remote(mass_all.at[0], mass_all.at[d], m2_s.at[d], m2_r.at[d], img_id(d))

    for du in [*range(1, outer), 0]:
        for dv in range(1, cores):
            for p in range(steps):
                core_send[du, dv - 1, p] = numer(slice_of(du, dv), p).astype(BF16)
                core_copy(du, dv, p).start()
        for p in range(steps):
            value = numer(slice_of(du, 0), p)
            for dv in range(1, cores):
                core_copy(du, dv, p).wait_recv()
                value += core_recv[du, dv - 1, p].astype(F32)
            if du:
                row_send[du - 1, p] = value.astype(BF16)
                if far > 1:
                    row_copy(du, p, True).start()
            else:
                own[p] = value
        if du:
            for p in range(steps):
                row_copy(du, p, False).start()
        if du == (1 if outer > 1 else 0):
            for b in range(near):
                mass += jnp.dot(
                    mass_sum[b], wide_marks[b * block : b * block + LANES, :].astype(F32),
                    precision=HIGHEST, preferred_element_type=F32,
                )
            mass_part[...] = mass.reshape(mass_part.shape)
            for d in range(1, far):
                mass_far(d).start()

    def far_copy(d, p):
        return remote(
            far_send.at[d, p], far_recv.at[d, p], f3_s.at[d, p], f3_r.at[d, p], far_id(d)
        )

    for p in range(steps):
        for du in range(1, outer):
            if far > 1:
                row_copy(du, p, True).wait_recv()
        for d in range(1, far):
            part = slice(d * classes, (d + 1) * classes)
            value = own[p, part]
            for du in range(1, outer):
                value += row_recv[du - 1, p, part].astype(F32)
            far_send[d, p] = value.astype(BF16)
            far_copy(d, p).start()

    value = mass_part[0]
    for d in range(1, far):
        mass_far(d).wait_recv()
        value += mass_recv[d]
    mass_all[0] = value
    for d in range(1, n_img):
        mass_img(d).start()

    for d in range(1, far):
        resp_far(d).wait_recv()
    resp_recv[0] = resp_send[0]
    pair = near * rows
    total = rows * n_cls
    for t in range(-(-total // LANES)):
        value = jnp.zeros((classes, LANES), F32)
        source = lane // pair + t * (LANES // pair)
        for j in range(far):
            value = jnp.where(source == lax.rem(q + j, far), resp_recv[j], value)
        width = min(LANES, total - t * LANES)
        resp_ref[:, t * LANES : t * LANES + width] = value[:, :width]

    for p in range(steps):
        for du in range(1, outer):
            row_copy(du, p, False).wait_recv()
            own[p, :classes] += row_recv[du - 1, p, :classes].astype(F32)

    for d in range(1, n_img):
        mass_img(d).wait_recv()
    mass = mass_all[0]
    for d in range(1, n_img):
        mass += mass_all[d]
    mine = pl.ds(freq_at(my_img, 0), part_freq)
    ctf = ctf_ref[:, mine]
    denom = jnp.dot(
        mass[:, :groups], ctf * ctf * nw_ref[:, mine], precision=HIGHEST,
        preferred_element_type=F32,
    ) + prior_precision

    for p in range(steps):
        value = own[p, :classes]
        for d in range(1, far):
            far_copy(d, p).wait_recv()
            value += far_recv[d, p].astype(F32)
        cols = slice(p * chunk, (p + 1) * chunk)
        for part in range(2):
            avg_ref[:, part, cols] = value[:, part * chunk : (part + 1) * chunk] / denom[:, cols]

    for d in range(1, near):
        stat_near(d).wait_send()
        marks_near(d).wait_send()
        for p in range(steps):
            w_near(d, p).wait_send()
    for d in range(1, far):
        power_far(d).wait_send()
        resp_far(d).wait_send()
        mass_far(d).wait_send()
        for p in range(steps):
            cls_far(d, p).wait_send()
            far_copy(d, p).wait_send()
            for e in range(1, n_img):
                cls_forward(d, p, e, my_img).wait_send()
    for d in range(1, n_img):
        mass_img(d).wait_send()
    for p in range(steps):
        for du in range(outer):
            for dv in range(1, cores):
                core_copy(du, dv, p).wait_send()
            if du:
                row_copy(du, p, False).wait_send()
                if far > 1:
                    row_copy(du, p, True).wait_send()


def local(n_cls, n_img, particles, classes, ctf, noise_weight, group_ids, shifts):
    rows, _, freq = particles.shape
    cls_rows = classes.shape[0]
    poses = shifts.shape[0]
    groups = ctf.shape[0]
    total = rows * n_cls
    part_freq = freq // n_img
    chunk = 384 if part_freq % 384 == 0 else LANES
    pad_groups = -(-groups // LANES) * LANES
    near = 2 if n_cls % 2 == 0 else 1
    cores = 2 if n_img % 2 == 0 else 1
    far = n_cls // near
    outer = n_img // cores
    steps = part_freq // chunk
    held = far * cls_rows
    wide = 2 * chunk
    block = poses * rows
    vmem = pl.BlockSpec(memory_space=pltpu.VMEM)
    dma = pltpu.SemaphoreType.DMA
    most = max(1, outer - 1)
    scratch = [
        ((rows, 2, freq), BF16),
        ((far, cls_rows, 2, freq), BF16),
        ((groups, freq), F32),
        ((1, freq), F32),
        ((rows, freq), F32),
        ((rows, pad_groups), F32),
        ((near, rows, pad_groups), BF16),
        ((near * block, pad_groups), BF16),
        ((poses, freq), F32),
        ((poses, freq), F32),
        ((steps, near, rows, n_img * wide), BF16),
        ((steps, near * block, n_img * wide), BF16),
        ((held, n_img * wide), BF16),
        ((far, cls_rows, pad_groups), F32),
        ((held, near * block), F32),
        ((held, near * block), BF16),
        ((near, -(-2 * near // 8) * 8, LANES), F32),
        ((far, cls_rows, LANES), F32),
        ((far, cls_rows, LANES), F32),
        ((far, cls_rows, pad_groups), F32),
        ((far, cls_rows, pad_groups), F32),
        ((n_img, cls_rows, pad_groups), F32),
        ((outer, max(1, cores - 1), steps, held, wide), BF16),
        ((outer, max(1, cores - 1), steps, held, wide), BF16),
        ((most, steps, held, wide), BF16),
        ((most, steps, held, wide), BF16),
        ((far, steps, cls_rows, wide), BF16),
        ((far, steps, cls_rows, wide), BF16),
        ((steps, held, wide), F32),
    ]
    sems = [(far, steps), (far, steps, n_img), (near, steps), (near,), (far,), (near,), (far,), (far,), (n_img,)]
    sems += [(outer, cores, steps), (outer, steps), (outer, steps), (far, steps)]
    resp, avg = pl.pallas_call(
        functools.partial(kernel, n_cls, n_img, near, cores, chunk),
        out_shape=(
            jax.ShapeDtypeStruct((cls_rows, total), F32),
            jax.ShapeDtypeStruct((cls_rows, 2, part_freq), F32),
        ),
        in_specs=[pl.BlockSpec(memory_space=pltpu.SMEM)] * 2
        + [pl.BlockSpec(memory_space=pl.ANY)] * 4,
        out_specs=(vmem, vmem),
        scratch_shapes=[pltpu.VMEM(*s) for s in scratch]
        + [dma((4,))]
        + [dma(s) for s in sems for _ in range(2)],
        compiler_params=pltpu.CompilerParams(
            collective_id=0, has_side_effects=True, vmem_limit_bytes=60 << 20
        ),
    )(
        group_ids,
        shifts.T,
        particles,
        classes,
        ctf,
        noise_weight,
    )
    return resp.T, avg


def solution(mesh):
    placed = (
        P(("groups", "img", "cls"), None, None),
        P(("groups", "cls"), None, None),
        P("groups", None),
        P("groups"),
        P(("groups", "img", "cls")),
        P("groups", None),
    )
    return jax.shard_map(
        functools.partial(local, mesh.shape["cls"], mesh.shape["img"]),
        mesh=mesh,
        in_specs=placed,
        out_specs=(P(("groups", "img"), "cls"), P(("groups", "cls"), None, "img")),
        check_vma=False,
    )
```

```python
import functools

import jax
import jax.numpy as jnp
from jax import lax
from jax.experimental import pallas as pl
from jax.experimental.pallas import tpu as pltpu
from jax.sharding import PartitionSpec as P

BOX = 128
LANES = 128
MESH = pl.DeviceIdType.MESH
HIGHEST = lax.Precision.HIGHEST
NT = (((1,), (1,)), ((), ()))
F32 = jnp.float32
BF16 = jnp.bfloat16

prior_precision = 0.02


def fill_phase_tables(shift_ref, cos_ref, sin_ref):
    poses, freq = cos_ref.shape
    step = 2.0 * jnp.pi / BOX
    lane = lax.broadcasted_iota(jnp.int32, (poses, BOX), 1)
    pose = lax.broadcasted_iota(jnp.int32, (poses, BOX), 0)
    move_x = jnp.zeros((poses, BOX), jnp.int32)
    move_y = jnp.zeros((poses, BOX), jnp.int32)
    for r in range(poses):
        move_x = jnp.where(pose == r, shift_ref[0, r], move_x)
        move_y = jnp.where(pose == r, shift_ref[1, r], move_y)
    move_x, move_y = move_x.astype(jnp.float32), move_y.astype(jnp.float32)
    angle_x = step * (move_x * (lane - BOX // 2).astype(jnp.float32))
    cos_x, sin_x = jnp.cos(angle_x), jnp.sin(angle_x)
    for row in range(freq // BOX):
        if row % BOX == 0:
            angle_y = step * (move_y * (lane + row).astype(jnp.float32))
            cos_rows, sin_rows = jnp.cos(angle_y), jnp.sin(angle_y)
        cos_y = cos_rows[:, row % BOX : row % BOX + 1]
        sin_y = sin_rows[:, row % BOX : row % BOX + 1]
        cols = slice(row * BOX, (row + 1) * BOX)
        cos_ref[:, cols] = cos_x * cos_y - sin_x * sin_y
        sin_ref[:, cols] = sin_x * cos_y + cos_x * sin_y


def kernel(
    n_cls, n_img, near, cores, chunk,
    ids_s, shift_ref, part_hbm, cls_hbm, ctf_hbm, nw_hbm,
    resp_ref, avg_ref,
    part_ref, cls_raw, ctf_ref, nw_ref, sel, onehot, marks, wide_marks, cos_ref, sin_ref,
    wbuf, turned, cls_mat, power_rows, power_buf, partial, scores, rho_low, stat, resp_send, resp_recv,
    mass_part, mass_recv, mass_all,
    core_send, core_recv, row_send, row_recv, far_recv, own,
    in_sem, cl_sem, cq_s, cq_r, cf_s, cf_r, wh_s, wh_r, mk_s, mk_r, pw_s, pw_r, st_s, st_r, rp_s, rp_r,
    m1_s, m1_r, m2_s, m2_r, c1_s, c1_r, r2_s, r2_r, o2_s, o2_r, f3_s, f3_r,
):
    rows = part_ref.shape[0]
    freq = ctf_ref.shape[1]
    groups = ctf_ref.shape[0]
    classes = cls_raw.shape[3]
    poses = cos_ref.shape[0]
    far = n_cls // near
    outer = n_img // cores
    part_freq = freq // n_img
    steps = part_freq // chunk
    wide = 2 * chunk
    block = poses * rows
    held = far * classes
    my_cls = lax.axis_index("cls")
    my_img = lax.axis_index("img")
    q, h = my_cls // near, lax.rem(my_cls, near)
    u, v = my_img // cores, lax.rem(my_img, cores)

    def near_id(d):
        return {"cls": q * near + lax.rem(h + d, near)}

    def far_id(d):
        return {"cls": lax.rem(q + d, far) * near + h}

    def img_id(d):
        return {"img": lax.rem(my_img + d, n_img)}

    def core_id(d):
        return {"img": u * cores + lax.rem(v + d, cores)}

    def outer_id(d):
        return {"img": lax.rem(u + d, outer) * cores + v}

    def remote(src, dst, send, recv, device):
        return pltpu.make_async_remote_copy(
            src_ref=src, dst_ref=dst, send_sem=send, recv_sem=recv,
            device_id=device, device_id_type=MESH,
        )

    barrier = pltpu.get_barrier_semaphore()
    peers = (
        [near_id(d) for d in range(1, near)]
        + [far_id(d) for d in range(1, far)]
        + [img_id(d) for d in range(1, n_img)]
    )
    for peer in peers:
        pl.semaphore_signal(barrier, inc=1, device_id=peer, device_id_type=MESH)

    def freq_at(img, p):
        return pl.multiple_of(img * part_freq + p * chunk, LANES)

    def cls_load(e, p):
        img = lax.rem(my_img + e, n_img)
        return pltpu.make_async_copy(
            cls_hbm.at[:, :, pl.ds(freq_at(img, p), chunk)], cls_raw.at[0, p, img], cl_sem.at[e, p]
        )

    inputs = [
        pltpu.make_async_copy(src, dst, in_sem.at[i])
        for i, (src, dst) in enumerate(
            ((ctf_hbm, ctf_ref), (nw_hbm, nw_ref.at[0]), (part_hbm, part_ref))
        )
    ]
    for p in range(steps):
        cls_load(0, p).start()
    for copy in inputs:
        copy.start()
    for e in range(1, n_img):
        for p in range(steps):
            cls_load(e, p).start()

    def cls_far(d, p):
        return remote(
            cls_raw.at[0, p, my_img], cls_raw.at[far - d, p, my_img],
            cq_s.at[d, p], cq_r.at[d, p], far_id(d),
        )

    def cls_forward(j, p, e, img):
        piece = cls_raw.at[j, p, img]
        return remote(piece, piece, cf_s.at[j, p, e], cf_r.at[j, p, e], img_id(e))

    def w_near(d, p):
        return remote(
            wbuf.at[p, 0], wbuf.at[p, near - d], wh_s.at[d, p], wh_r.at[d, p], near_id(d)
        )

    def marks_near(d):
        return remote(marks.at[0], marks.at[near - d], mk_s.at[d], mk_r.at[d], near_id(d))

    def power_far(d):
        return remote(
            power_buf.at[0], power_buf.at[far - d], pw_s.at[d], pw_r.at[d], far_id(d)
        )

    pl.semaphore_wait(barrier, len(peers))
    for p in range(steps):
        cls_load(0, p).wait()
        for d in range(1, far):
            cls_far(d, p).start()

    for copy in inputs:
        copy.wait()
    for i in range(rows):
        sel[pl.ds(i, 1), :] = ctf_ref[pl.ds(ids_s[i], 1), :] * nw_ref[...]
        onehot[pl.ds(i, 1), :] = (
            lax.broadcasted_iota(jnp.int32, (1, onehot.shape[1]), 1) == ids_s[i]
        ).astype(F32)
    for p in range(steps):
        for i in range(n_img):
            cols = slice(i * part_freq + p * chunk, i * part_freq + (p + 1) * chunk)
            for part in range(2):
                at = i * wide + part * chunk
                wbuf[p, 0, :, at : at + chunk] = (
                    part_ref[:, part, cols].astype(F32) * sel[:, cols]
                ).astype(BF16)
        for d in range(1, near):
            w_near(d, p).start()
    marks[0] = onehot[...].astype(BF16)
    for d in range(1, near):
        marks_near(d).start()

    fill_phase_tables(shift_ref, cos_ref, sin_ref)

    half = n_img * chunk

    def turn(p, b):
        def one(i, carry):
            at = pl.ds(freq_at(i, p), chunk)
            re_from = pl.ds(pl.multiple_of(i * wide, LANES), chunk)
            im_from = pl.ds(pl.multiple_of(i * wide + chunk, LANES), chunk)
            re_at = pl.ds(pl.multiple_of(i * chunk, LANES), chunk)
            im_at = pl.ds(pl.multiple_of(half + i * chunk, LANES), chunk)
            re = wbuf[p, b, :, re_from].astype(F32)
            im = wbuf[p, b, :, im_from].astype(F32)
            for r in range(poses):
                cos_r = cos_ref[r : r + 1, at]
                sin_r = sin_ref[r : r + 1, at]
                out = slice(b * block + r * rows, b * block + (r + 1) * rows)
                turned[p, out, re_at] = (re * cos_r + im * sin_r).astype(BF16)
                turned[p, out, im_at] = (im * cos_r - re * sin_r).astype(BF16)
            return carry

        lax.fori_loop(0, n_img, one, 0)

    by_distance = sorted(range(1, n_img), key=lambda e: e % cores == 0, reverse=True)

    def relay(p):
        for d in range(1, far):
            cls_far(d, p).wait_recv()
            for e in by_distance:
                cls_forward(far - d, p, e, my_img).start()

    for p in range(steps):
        turn(p, 0)
        if p == min(1, steps - 1):
            relay(0)
    for e in range(1, n_img):
        for p in range(steps):
            cls_load(e, p).wait()

    def halves(x):
        top = x.astype(BF16)
        return jnp.concatenate([top, (x - top.astype(F32)).astype(BF16)], axis=0)

    def power_step(p, total):
        for i in range(n_img):
            at = pl.ds(freq_at(i, p), chunk)
            value = cls_raw[0, p, i].reshape(2 * classes, chunk).astype(F32)
            ctf = ctf_ref[:, at]
            total += lax.dot_general(
                halves(value * value), halves(ctf * ctf * nw_ref[:, at]), NT,
                preferred_element_type=F32,
            )
        return total

    if steps > 1:
        relay(1)
    power = lax.fori_loop(0, steps, power_step, jnp.zeros((4 * classes, 2 * groups), F32))
    power_rows[...] = jnp.zeros_like(power_rows)
    power_rows[:, :groups] = (
        power[: 2 * classes, :groups] + power[: 2 * classes, groups:] + power[2 * classes :, :groups]
    )
    power_buf[0] = (
        power_rows[pl.ds(0, classes, stride=2), :] + power_rows[pl.ds(1, classes, stride=2), :]
    )
    for d in range(1, far):
        power_far(d).start()
    def turn_near(p):
        for d in range(1, near):
            w_near(d, p).wait_recv()
            turn(p, near - d)

    turn_near(0)
    if steps > 2:
        relay(2)

    tiles = block // LANES

    def match(p, b):
        row = lax.broadcasted_iota(jnp.int32, (2 * held, block), 0)
        pair = [
            lax.dot_general(
                cls_mat[...],
                turned[p, b * block : (b + 1) * block, part * half : (part + 1) * half],
                NT,
                preferred_element_type=F32,
            )
            for part in range(2)
        ]
        value = jnp.where(row % 2 == 0, pair[0], pair[1])
        for t in range(tiles):
            at = slice(t * LANES, (t + 1) * LANES)
            if p:
                partial[b * tiles + t] += value[:, at]
            else:
                partial[b * tiles + t] = value[:, at]

    def match_all(p):
        for j in range(1, far):
            for e in range(1, n_img):
                cls_forward(j, p, e, lax.rem(my_img + n_img - e, n_img)).wait_recv()

        def lay(i, carry):
            at = pl.ds(pl.multiple_of(i * chunk, LANES), chunk)
            for j in range(far):
                cls_mat[2 * j * classes : 2 * (j + 1) * classes, at] = cls_raw[j, p, i].reshape(
                    2 * classes, chunk
                )
            return carry

        lax.fori_loop(0, n_img, lay, 0)
        for b in range(near):
            match(p, b)

    def penalise():
        for d in range(1, near):
            marks_near(d).wait_recv()
        for b in range(near):
            for r in range(poses):
                wide_marks[b * block + r * rows : b * block + (r + 1) * rows, :] = marks[b]
        for d in range(1, far):
            power_far(d).wait_recv()
        rest = -0.5 * power_buf[...].reshape(held, power_buf.shape[2])
        penalty = jnp.zeros(scores.shape, F32)
        for _ in range(3):
            top = rest.astype(BF16)
            rest = rest - top.astype(F32)
            penalty += lax.dot_general(top, wide_marks[...], NT, preferred_element_type=F32)
        scores[...] = penalty

    for p in range(steps):
        if p:
            turn_near(p)
        if p == steps - 1:
            penalise()
        if p > 2:
            relay(p)
        match_all(p)

    for k in range(near * tiles):
        at = slice(k * LANES, (k + 1) * LANES)
        scores[:, at] += (
            partial[k, pl.ds(0, held, stride=2), :] + partial[k, pl.ds(1, held, stride=2), :]
        )


    def over_poses(op, pieces):
        value = functools.reduce(op, pieces)
        shift = LANES // 2
        while shift >= rows:
            value = op(value, pltpu.roll(value, shift, 1))
            shift //= 2
        return value

    def tile(b, t):
        return slice(b * block + t * LANES, b * block + (t + 1) * LANES)

    pose_peak, pose_sum, peak, mass_sum = [], [], [], []
    for b in range(near):
        top = over_poses(jnp.maximum, [scores[:, tile(b, t)] for t in range(tiles)])
        total = over_poses(jnp.add, [jnp.exp(scores[:, tile(b, t)] - top) for t in range(tiles)])
        whole = jnp.max(top, axis=0, keepdims=True)
        pose_peak.append(top)
        pose_sum.append(total)
        peak.append(whole)
        mass_sum.append(jnp.sum(total * jnp.exp(top - whole), axis=0, keepdims=True))
        stat[0, b : b + 1, :] = whole
        stat[0, near + b : near + b + 1, :] = mass_sum[b]

    def stat_near(d):
        return remote(stat.at[0], stat.at[d], st_s.at[d], st_r.at[d], near_id(d))

    for d in range(1, near):
        stat_near(d).start()
    log_sums = [pose_peak[b] + jnp.log(pose_sum[b]) for b in range(near)]
    for d in range(1, near):
        stat_near(d).wait_recv()
    mass = jnp.zeros((held, marks.shape[2]), F32)
    lane = lax.broadcasted_iota(jnp.int32, (1, LANES), 1)
    lane_h = lax.rem(lane // rows, near)
    both = jnp.zeros((held, LANES), F32)
    for b in range(near):
        tops = [stat[d, (b + d) % near : (b + d) % near + 1, :] for d in range(near)]
        sums = [stat[d, near + (b + d) % near : near + (b + d) % near + 1, :] for d in range(near)]
        whole = functools.reduce(jnp.maximum, tops)
        norm = functools.reduce(jnp.add, [s * jnp.exp(t - whole) for s, t in zip(sums, tops)])
        log_norm = whole + jnp.log(norm)
        for t in range(tiles):
            rho_low[:, tile(b, t)] = jnp.exp(scores[:, tile(b, t)] - log_norm).astype(BF16)
        pose_total = pose_sum[b] * jnp.exp(pose_peak[b] - log_norm)
        mass_sum[b] = jnp.where(lane < rows, pose_total, 0.0)
        both = jnp.where(lane_h == lax.rem(h + b, near), log_sums[b] - log_norm, both)
    resp_send[...] = both.reshape(resp_send.shape)

    def resp_far(d):
        return remote(resp_send.at[d], resp_recv.at[far - d], rp_s.at[d], rp_r.at[d], far_id(d))

    for d in range(1, far):
        resp_far(d).start()

    def numer(du, part, p):
        width = cores * chunk
        at = pl.multiple_of(part * half + lax.rem(u + du, outer) * width, LANES)
        value = jnp.dot(
            rho_low[...], turned[p, :, pl.ds(at, width)], preferred_element_type=F32
        )
        pieces = [value[:, c * chunk : (c + 1) * chunk] for c in range(cores)]

        def piece(dv):
            chosen = pieces[0]
            for c in range(1, cores):
                chosen = jnp.where(lax.rem(v + dv, cores) == c, pieces[c], chosen)
            return chosen

        return [piece(dv) for dv in range(cores)]

    def core_copy(du, dv, p):
        return remote(
            core_send.at[du, dv - 1, p], core_recv.at[du, dv - 1, p],
            c1_s.at[du, dv, p], c1_r.at[du, dv, p], core_id(dv),
        )

    def row_copy(du, p, theirs):
        part = pl.ds(classes, held - classes) if theirs else pl.ds(0, classes)
        send, recv = (r2_s, r2_r) if theirs else (o2_s, o2_r)
        return remote(
            row_send.at[du - 1, p, part], row_recv.at[du - 1, p, part],
            send.at[du, p], recv.at[du, p], outer_id(du),
        )

    def mass_far(d):
        return remote(
            mass_part.at[d], mass_recv.at[d], m1_s.at[d], m1_r.at[d], far_id(d)
        )

    def mass_img(d):
        return remote(mass_all.at[0], mass_all.at[d], m2_s.at[d], m2_r.at[d], img_id(d))

    for du in [*range(1, outer), 0]:
        for p in range(steps):
            for part in range(2):
                cols = slice(part * chunk, (part + 1) * chunk)
                mine, *theirs = numer(du, part, p)
                own[p, :, cols] = mine
                for dv in range(1, cores):
                    core_send[du, dv - 1, p, :, cols] = theirs[dv - 1].astype(BF16)
            for dv in range(1, cores):
                core_copy(du, dv, p).start()
        for p in range(steps):
            value = own[p]
            for dv in range(1, cores):
                core_copy(du, dv, p).wait_recv()
                value += core_recv[du, dv - 1, p].astype(F32)
            if du:
                row_send[du - 1, p] = value.astype(BF16)
                if far > 1:
                    row_copy(du, p, True).start()
            else:
                own[p] = value
        if du:
            for p in range(steps):
                row_copy(du, p, False).start()
        if du == (1 if outer > 1 else 0):
            for b in range(near):
                mass += jnp.dot(
                    mass_sum[b], wide_marks[b * block : b * block + LANES, :].astype(F32),
                    precision=HIGHEST, preferred_element_type=F32,
                )
            mass_part[...] = mass.reshape(mass_part.shape)
            for d in range(1, far):
                mass_far(d).start()

    def far_copy(d, p):
        return remote(
            core_send.at[0, 0, p, pl.ds(d * classes, classes)], far_recv.at[d, p], f3_s.at[d, p], f3_r.at[d, p], far_id(d)
        )

    for p in range(steps):
        for dv in range(1, cores):
            core_copy(0, dv, p).wait_send()
        for du in range(1, outer):
            if far > 1:
                row_copy(du, p, True).wait_recv()
        for d in range(1, far):
            part = slice(d * classes, (d + 1) * classes)
            value = own[p, part]
            for du in range(1, outer):
                value += row_recv[du - 1, p, part].astype(F32)
            core_send[0, 0, p, part] = value.astype(BF16)
            far_copy(d, p).start()

    value = mass_part[0]
    for d in range(1, far):
        mass_far(d).wait_recv()
        value += mass_recv[d]
    mass_all[0] = value
    for d in range(1, n_img):
        mass_img(d).start()

    for d in range(1, far):
        resp_far(d).wait_recv()
    resp_recv[0] = resp_send[0]
    pair = near * rows
    total = rows * n_cls
    for t in range(-(-total // LANES)):
        value = jnp.zeros((classes, LANES), F32)
        source = lane // pair + t * (LANES // pair)
        for j in range(far):
            value = jnp.where(source == lax.rem(q + j, far), resp_recv[j], value)
        width = min(LANES, total - t * LANES)
        resp_ref[:, t * LANES : t * LANES + width] = value[:, :width]

    for p in range(steps):
        for du in range(1, outer):
            row_copy(du, p, False).wait_recv()
            own[p, :classes] += row_recv[du - 1, p, :classes].astype(F32)

    for d in range(1, n_img):
        mass_img(d).wait_recv()
    mass = mass_all[0]
    for d in range(1, n_img):
        mass += mass_all[d]
    mine = pl.ds(freq_at(my_img, 0), part_freq)
    ctf = ctf_ref[:, mine]
    denom = jnp.dot(
        mass[:, :groups], ctf * ctf * nw_ref[:, mine], precision=HIGHEST,
        preferred_element_type=F32,
    ) + prior_precision

    for p in range(steps):
        value = own[p, :classes]
        for d in range(1, far):
            far_copy(d, p).wait_recv()
            value += far_recv[d, p].astype(F32)
        cols = slice(p * chunk, (p + 1) * chunk)
        for part in range(2):
            avg_ref[:, part, cols] = value[:, part * chunk : (part + 1) * chunk] / denom[:, cols]

    for d in range(1, near):
        stat_near(d).wait_send()
        marks_near(d).wait_send()
        for p in range(steps):
            w_near(d, p).wait_send()
    for d in range(1, far):
        power_far(d).wait_send()
        resp_far(d).wait_send()
        mass_far(d).wait_send()
        for p in range(steps):
            cls_far(d, p).wait_send()
            far_copy(d, p).wait_send()
            for e in range(1, n_img):
                cls_forward(d, p, e, my_img).wait_send()
    for d in range(1, n_img):
        mass_img(d).wait_send()
    for p in range(steps):
        for du in range(outer):
            if du:
                for dv in range(1, cores):
                    core_copy(du, dv, p).wait_send()
                row_copy(du, p, False).wait_send()
                if far > 1:
                    row_copy(du, p, True).wait_send()


def settle_kernel(resp_from, avg_from, resp_to, avg_to):
    resp_to[...] = resp_from[...]
    avg_to[...] = avg_from[...]


def settle(resp, avg):
    vmem = pl.BlockSpec(memory_space=pltpu.VMEM)
    return pl.pallas_call(
        settle_kernel,
        out_shape=tuple(jax.ShapeDtypeStruct(x.shape, x.dtype) for x in (resp, avg)),
        in_specs=[vmem] * 2,
        out_specs=(vmem, vmem),
    )(resp, avg)


def local(n_cls, n_img, particles, classes, ctf, noise_weight, group_ids, shifts):
    rows, _, freq = particles.shape
    cls_rows = classes.shape[0]
    poses = shifts.shape[0]
    groups = ctf.shape[0]
    total = rows * n_cls
    part_freq = freq // n_img
    chunk = 384 if part_freq % 384 == 0 else LANES
    pad_groups = -(-groups // LANES) * LANES
    near = 2 if n_cls % 2 == 0 else 1
    cores = 2 if n_img % 2 == 0 else 1
    far = n_cls // near
    outer = n_img // cores
    steps = part_freq // chunk
    held = far * cls_rows
    wide = 2 * chunk
    block = poses * rows
    vmem = pl.BlockSpec(memory_space=pltpu.VMEM)
    dma = pltpu.SemaphoreType.DMA
    most = max(1, outer - 1)
    scratch = [
        ((rows, 2, freq), BF16),
        ((far, steps, n_img, cls_rows, 2, chunk), BF16),
        ((groups, freq), F32),
        ((1, freq), F32),
        ((rows, freq), F32),
        ((rows, pad_groups), F32),
        ((near, rows, pad_groups), BF16),
        ((near * block, pad_groups), BF16),
        ((poses, freq), F32),
        ((poses, freq), F32),
        ((steps, near, rows, n_img * wide), BF16),
        ((steps, near * block, n_img * wide), BF16),
        ((2 * held, n_img * chunk), BF16),
        ((2 * cls_rows, pad_groups), F32),
        ((far, cls_rows, pad_groups), F32),
        ((near * block // LANES, 2 * held, LANES), F32),
        ((held, near * block), F32),
        ((held, near * block), BF16),
        ((near, -(-2 * near // 8) * 8, LANES), F32),
        ((far, cls_rows, LANES), F32),
        ((far, cls_rows, LANES), F32),
        ((far, cls_rows, pad_groups), F32),
        ((far, cls_rows, pad_groups), F32),
        ((n_img, cls_rows, pad_groups), F32),
        ((outer, max(1, cores - 1), steps, held, wide), BF16),
        ((outer, max(1, cores - 1), steps, held, wide), BF16),
        ((most, steps, held, wide), BF16),
        ((most, steps, held, wide), BF16),
        ((far, steps, cls_rows, wide), BF16),
        ((steps, held, wide), F32),
    ]
    sems = [(far, steps), (far, steps, n_img), (near, steps), (near,), (far,), (near,), (far,), (far,), (n_img,)]
    sems += [(outer, cores, steps), (outer, steps), (outer, steps), (far, steps)]
    resp, avg = pl.pallas_call(
        functools.partial(kernel, n_cls, n_img, near, cores, chunk),
        out_shape=(
            jax.ShapeDtypeStruct((cls_rows, total), F32),
            jax.ShapeDtypeStruct((cls_rows, 2, part_freq), F32),
        ),
        in_specs=[pl.BlockSpec(memory_space=pltpu.SMEM)] * 2
        + [pl.BlockSpec(memory_space=pl.ANY)] * 4,
        out_specs=(vmem, vmem),
        scratch_shapes=[pltpu.VMEM(*s) for s in scratch]
        + [dma((3,)), dma((n_img, steps))]
        + [dma(s) for s in sems for _ in range(2)],
        compiler_params=pltpu.CompilerParams(
            collective_id=0, has_side_effects=True, vmem_limit_bytes=61 << 20
        ),
    )(
        group_ids,
        shifts.T,
        particles,
        classes,
        ctf,
        noise_weight,
    )
    resp, avg = settle(resp, avg)
    return resp.T, avg


def solution(mesh):
    placed = (
        P(("groups", "img", "cls"), None, None),
        P(("groups", "cls"), None, None),
        P("groups", None),
        P("groups"),
        P(("groups", "img", "cls")),
        P("groups", None),
    )
    return jax.shard_map(
        functools.partial(local, mesh.shape["cls"], mesh.shape["img"]),
        mesh=mesh,
        in_specs=placed,
        out_specs=(P(("groups", "img"), "cls"), P(("groups", "cls"), None, "img")),
        check_vma=False,
    )
```

```python
import functools

import jax
import jax.numpy as jnp
from jax import lax
from jax.experimental import pallas as pl
from jax.experimental.pallas import tpu as pltpu
from jax.sharding import PartitionSpec as P

BOX = 128
LANES = 128
MESH = pl.DeviceIdType.MESH
HIGHEST = lax.Precision.HIGHEST
NT = (((1,), (1,)), ((), ()))
F32 = jnp.float32
BF16 = jnp.bfloat16

prior_precision = 0.02


def fill_phase_tables(shift_ref, cos_ref, sin_ref):
    poses, freq = cos_ref.shape
    step = 2.0 * jnp.pi / BOX
    lane = lax.broadcasted_iota(jnp.int32, (poses, BOX), 1)
    pose = lax.broadcasted_iota(jnp.int32, (poses, BOX), 0)
    move_x = jnp.zeros((poses, BOX), jnp.int32)
    move_y = jnp.zeros((poses, BOX), jnp.int32)
    for r in range(poses):
        move_x = jnp.where(pose == r, shift_ref[0, r], move_x)
        move_y = jnp.where(pose == r, shift_ref[1, r], move_y)
    move_x, move_y = move_x.astype(jnp.float32), move_y.astype(jnp.float32)
    angle_x = step * (move_x * (lane - BOX // 2).astype(jnp.float32))
    cos_x, sin_x = jnp.cos(angle_x), jnp.sin(angle_x)
    for row in range(freq // BOX):
        if row % BOX == 0:
            angle_y = step * (move_y * (lane + row).astype(jnp.float32))
            cos_rows, sin_rows = jnp.cos(angle_y), jnp.sin(angle_y)
        cos_y = cos_rows[:, row % BOX : row % BOX + 1]
        sin_y = sin_rows[:, row % BOX : row % BOX + 1]
        cols = slice(row * BOX, (row + 1) * BOX)
        cos_ref[:, cols] = cos_x * cos_y - sin_x * sin_y
        sin_ref[:, cols] = sin_x * cos_y + cos_x * sin_y


def kernel(
    n_cls, n_img, near, cores, chunk,
    ids_s, shift_ref, part_hbm, cls_hbm, ctf_hbm, nw_hbm,
    resp_ref, avg_ref,
    part_ref, cls_raw, ctf_ref, nw_ref, sel, onehot, marks, wide_marks, cos_ref, sin_ref,
    wbuf, turned, cls_mat, power_rows, power_buf, partial, scores, rho_low, stat, resp_send, resp_recv,
    mass_part, mass_recv, mass_all,
    core_send, core_recv, row_send, row_recv, far_recv, own,
    in_sem, cl_sem, cq_s, cq_r, cf_s, cf_r, wh_s, wh_r, mk_s, mk_r, pw_s, pw_r, st_s, st_r, rp_s, rp_r,
    m1_s, m1_r, m2_s, m2_r, c1_s, c1_r, r2_s, r2_r, o2_s, o2_r, f3_s, f3_r,
):
    rows = part_ref.shape[0]
    freq = ctf_ref.shape[1]
    groups = ctf_ref.shape[0]
    classes = cls_raw.shape[3]
    poses = cos_ref.shape[0]
    far = n_cls // near
    outer = n_img // cores
    part_freq = freq // n_img
    steps = part_freq // chunk
    wide = 2 * chunk
    block = poses * rows
    held = far * classes
    my_cls = lax.axis_index("cls")
    my_img = lax.axis_index("img")
    q, h = my_cls // near, lax.rem(my_cls, near)
    u, v = my_img // cores, lax.rem(my_img, cores)

    def near_id(d):
        return {"cls": q * near + lax.rem(h + d, near)}

    def far_id(d):
        return {"cls": lax.rem(q + d, far) * near + h}

    def img_id(d):
        return {"img": lax.rem(my_img + d, n_img)}

    def core_id(d):
        return {"img": u * cores + lax.rem(v + d, cores)}

    def outer_id(d):
        return {"img": lax.rem(u + d, outer) * cores + v}

    def remote(src, dst, send, recv, device):
        return pltpu.make_async_remote_copy(
            src_ref=src, dst_ref=dst, send_sem=send, recv_sem=recv,
            device_id=device, device_id_type=MESH,
        )

    barrier = pltpu.get_barrier_semaphore()
    peers = (
        [near_id(d) for d in range(1, near)]
        + [far_id(d) for d in range(1, far)]
        + [img_id(d) for d in range(1, n_img)]
    )
    for peer in peers:
        pl.semaphore_signal(barrier, inc=1, device_id=peer, device_id_type=MESH)

    def freq_at(img, p):
        return pl.multiple_of(img * part_freq + p * chunk, LANES)

    def cls_load(e, p):
        img = lax.rem(my_img + e, n_img)
        return pltpu.make_async_copy(
            cls_hbm.at[:, :, pl.ds(freq_at(img, p), chunk)], cls_raw.at[0, p, img], cl_sem.at[e, p]
        )

    inputs = [
        pltpu.make_async_copy(src, dst, in_sem.at[i])
        for i, (src, dst) in enumerate(
            ((ctf_hbm, ctf_ref), (nw_hbm, nw_ref.at[0]), (part_hbm, part_ref))
        )
    ]
    for p in range(steps):
        cls_load(0, p).start()
    for copy in inputs:
        copy.start()
    for e in range(1, n_img):
        for p in range(steps):
            cls_load(e, p).start()

    def cls_far(d, p):
        return remote(
            cls_raw.at[0, p, my_img], cls_raw.at[far - d, p, my_img],
            cq_s.at[d, p], cq_r.at[d, p], far_id(d),
        )

    def cls_forward(j, p, e, img):
        piece = cls_raw.at[j, p, img]
        return remote(piece, piece, cf_s.at[j, p, e], cf_r.at[j, p, e], img_id(e))

    def w_near(d, p):
        return remote(
            wbuf.at[p, 0], wbuf.at[p, near - d], wh_s.at[d, p], wh_r.at[d, p], near_id(d)
        )

    def marks_near(d):
        return remote(marks.at[0], marks.at[near - d], mk_s.at[d], mk_r.at[d], near_id(d))

    def power_far(d):
        return remote(
            power_buf.at[0], power_buf.at[far - d], pw_s.at[d], pw_r.at[d], far_id(d)
        )

    pl.semaphore_wait(barrier, len(peers))
    for p in range(steps):
        cls_load(0, p).wait()
        for d in range(1, far):
            cls_far(d, p).start()

    for copy in inputs:
        copy.wait()
    for i in range(rows):
        sel[pl.ds(i, 1), :] = ctf_ref[pl.ds(ids_s[i], 1), :] * nw_ref[...]
        onehot[pl.ds(i, 1), :] = (
            lax.broadcasted_iota(jnp.int32, (1, onehot.shape[1]), 1) == ids_s[i]
        ).astype(F32)
    for p in range(steps):
        for i in range(n_img):
            cols = slice(i * part_freq + p * chunk, i * part_freq + (p + 1) * chunk)
            for part in range(2):
                at = i * wide + part * chunk
                wbuf[p, 0, :, at : at + chunk] = (
                    part_ref[:, part, cols].astype(F32) * sel[:, cols]
                ).astype(BF16)
        for d in range(1, near):
            w_near(d, p).start()
    marks[0] = onehot[...].astype(BF16)
    for d in range(1, near):
        marks_near(d).start()

    fill_phase_tables(shift_ref, cos_ref, sin_ref)

    half = n_img * chunk

    def turn(p, b):
        def one(i, carry):
            at = pl.ds(freq_at(i, p), chunk)
            re_from = pl.ds(pl.multiple_of(i * wide, LANES), chunk)
            im_from = pl.ds(pl.multiple_of(i * wide + chunk, LANES), chunk)
            re_at = pl.ds(pl.multiple_of(i * chunk, LANES), chunk)
            im_at = pl.ds(pl.multiple_of(half + i * chunk, LANES), chunk)
            re = wbuf[p, b, :, re_from].astype(F32)
            im = wbuf[p, b, :, im_from].astype(F32)
            for r in range(poses):
                cos_r = cos_ref[r : r + 1, at]
                sin_r = sin_ref[r : r + 1, at]
                out = slice(b * block + r * rows, b * block + (r + 1) * rows)
                turned[p, out, re_at] = (re * cos_r + im * sin_r).astype(BF16)
                turned[p, out, im_at] = (im * cos_r - re * sin_r).astype(BF16)
            return carry

        lax.fori_loop(0, n_img, one, 0)

    by_distance = sorted(range(1, n_img), key=lambda e: e % cores == 0, reverse=True)

    def relay(p):
        for d in range(1, far):
            cls_far(d, p).wait_recv()
            for e in by_distance:
                cls_forward(far - d, p, e, my_img).start()

    for p in range(steps):
        turn(p, 0)
        if p == min(1, steps - 1):
            relay(0)
    for e in range(1, n_img):
        for p in range(steps):
            cls_load(e, p).wait()

    def halves(x):
        top = x.astype(BF16)
        return jnp.concatenate([top, (x - top.astype(F32)).astype(BF16)], axis=0)

    def power_step(p, total):
        for i in range(n_img):
            at = pl.ds(freq_at(i, p), chunk)
            value = cls_raw[0, p, i].reshape(2 * classes, chunk).astype(F32)
            ctf = ctf_ref[:, at]
            total += lax.dot_general(
                halves(value * value), halves(ctf * ctf * nw_ref[:, at]), NT,
                preferred_element_type=F32,
            )
        return total

    if steps > 1:
        relay(1)
    power = lax.fori_loop(0, steps, power_step, jnp.zeros((4 * classes, 2 * groups), F32))
    power_rows[...] = jnp.zeros_like(power_rows)
    power_rows[:, :groups] = (
        power[: 2 * classes, :groups] + power[: 2 * classes, groups:] + power[2 * classes :, :groups]
    )
    power_buf[0] = (
        power_rows[pl.ds(0, classes, stride=2), :] + power_rows[pl.ds(1, classes, stride=2), :]
    )
    for d in range(1, far):
        power_far(d).start()
    def turn_near(p):
        for d in range(1, near):
            w_near(d, p).wait_recv()
            turn(p, near - d)

    turn_near(0)
    if steps > 2:
        relay(2)

    tiles = block // LANES

    def match(p, b):
        row = lax.broadcasted_iota(jnp.int32, (2 * held, block), 0)
        pair = [
            lax.dot_general(
                cls_mat[...],
                turned[p, b * block : (b + 1) * block, part * half : (part + 1) * half],
                NT,
                preferred_element_type=F32,
            )
            for part in range(2)
        ]
        value = jnp.where(row % 2 == 0, pair[0], pair[1])
        for t in range(tiles):
            at = slice(t * LANES, (t + 1) * LANES)
            if p:
                partial[b * tiles + t] += value[:, at]
            else:
                partial[b * tiles + t] = value[:, at]

    def match_all(p):
        for j in range(1, far):
            for e in range(1, n_img):
                cls_forward(j, p, e, lax.rem(my_img + n_img - e, n_img)).wait_recv()

        def lay(i, carry):
            at = pl.ds(pl.multiple_of(i * chunk, LANES), chunk)
            for j in range(far):
                cls_mat[2 * j * classes : 2 * (j + 1) * classes, at] = cls_raw[j, p, i].reshape(
                    2 * classes, chunk
                )
            return carry

        lax.fori_loop(0, n_img, lay, 0)
        for b in range(near):
            match(p, b)

    def penalise():
        for d in range(1, near):
            marks_near(d).wait_recv()
        for b in range(near):
            for r in range(poses):
                wide_marks[b * block + r * rows : b * block + (r + 1) * rows, :] = marks[b]
        for d in range(1, far):
            power_far(d).wait_recv()
        rest = -0.5 * power_buf[...].reshape(held, power_buf.shape[2])
        penalty = jnp.zeros(scores.shape, F32)
        for _ in range(3):
            top = rest.astype(BF16)
            rest = rest - top.astype(F32)
            penalty += lax.dot_general(top, wide_marks[...], NT, preferred_element_type=F32)
        scores[...] = penalty

    for p in range(steps):
        if p:
            turn_near(p)
        if p == steps - 1:
            penalise()
        if p > 2:
            relay(p)
        match_all(p)

    for k in range(near * tiles):
        at = slice(k * LANES, (k + 1) * LANES)
        scores[:, at] += (
            partial[k, pl.ds(0, held, stride=2), :] + partial[k, pl.ds(1, held, stride=2), :]
        )


    def over_poses(op, pieces):
        value = functools.reduce(op, pieces)
        shift = LANES // 2
        while shift >= rows:
            value = op(value, pltpu.roll(value, shift, 1))
            shift //= 2
        return value

    def tile(b, t):
        return slice(b * block + t * LANES, b * block + (t + 1) * LANES)

    pose_peak, pose_sum, peak, mass_sum = [], [], [], []
    for b in range(near):
        top = over_poses(jnp.maximum, [scores[:, tile(b, t)] for t in range(tiles)])
        total = over_poses(jnp.add, [jnp.exp(scores[:, tile(b, t)] - top) for t in range(tiles)])
        whole = jnp.max(top, axis=0, keepdims=True)
        pose_peak.append(top)
        pose_sum.append(total)
        peak.append(whole)
        mass_sum.append(jnp.sum(total * jnp.exp(top - whole), axis=0, keepdims=True))
        stat[0, b : b + 1, :] = whole
        stat[0, near + b : near + b + 1, :] = mass_sum[b]

    def stat_near(d):
        return remote(stat.at[0], stat.at[d], st_s.at[d], st_r.at[d], near_id(d))

    for d in range(1, near):
        stat_near(d).start()
    log_sums = [pose_peak[b] + jnp.log(pose_sum[b]) for b in range(near)]
    for d in range(1, near):
        stat_near(d).wait_recv()
    mass = jnp.zeros((held, marks.shape[2]), F32)
    lane = lax.broadcasted_iota(jnp.int32, (1, LANES), 1)
    lane_h = lax.rem(lane // rows, near)
    both = jnp.zeros((held, LANES), F32)
    for b in range(near):
        tops = [stat[d, (b + d) % near : (b + d) % near + 1, :] for d in range(near)]
        sums = [stat[d, near + (b + d) % near : near + (b + d) % near + 1, :] for d in range(near)]
        whole = functools.reduce(jnp.maximum, tops)
        norm = functools.reduce(jnp.add, [s * jnp.exp(t - whole) for s, t in zip(sums, tops)])
        log_norm = whole + jnp.log(norm)
        for t in range(tiles):
            rho_low[:, tile(b, t)] = jnp.exp(scores[:, tile(b, t)] - log_norm).astype(BF16)
        pose_total = pose_sum[b] * jnp.exp(pose_peak[b] - log_norm)
        mass_sum[b] = jnp.where(lane < rows, pose_total, 0.0)
        both = jnp.where(lane_h == lax.rem(h + b, near), log_sums[b] - log_norm, both)
    resp_send[...] = both.reshape(resp_send.shape)

    def resp_far(d):
        return remote(resp_send.at[d], resp_recv.at[far - d], rp_s.at[d], rp_r.at[d], far_id(d))

    for d in range(1, far):
        resp_far(d).start()

    def numer(du, part, p):
        width = cores * chunk
        at = pl.multiple_of(part * half + lax.rem(u + du, outer) * width, LANES)
        value = jnp.dot(
            rho_low[...], turned[p, :, pl.ds(at, width)], preferred_element_type=F32
        )
        pieces = [value[:, c * chunk : (c + 1) * chunk] for c in range(cores)]

        def piece(dv):
            chosen = pieces[0]
            for c in range(1, cores):
                chosen = jnp.where(lax.rem(v + dv, cores) == c, pieces[c], chosen)
            return chosen

        return [piece(dv) for dv in range(cores)]

    def core_copy(du, dv, p):
        return remote(
            core_send.at[du, dv - 1, p], core_recv.at[du, dv - 1, p],
            c1_s.at[du, dv, p], c1_r.at[du, dv, p], core_id(dv),
        )

    def row_copy(du, p, theirs):
        part = pl.ds(classes, held - classes) if theirs else pl.ds(0, classes)
        send, recv = (r2_s, r2_r) if theirs else (o2_s, o2_r)
        return remote(
            row_send.at[du - 1, p, part], row_recv.at[du - 1, p, part],
            send.at[du, p], recv.at[du, p], outer_id(du),
        )

    def mass_far(d):
        return remote(
            mass_part.at[d], mass_recv.at[d], m1_s.at[d], m1_r.at[d], far_id(d)
        )

    def mass_img(d):
        return remote(mass_all.at[0], mass_all.at[d], m2_s.at[d], m2_r.at[d], img_id(d))

    def slot(du, p):
        if du:
            return (du - 1) * steps + p
        return max(1, outer - 1) * steps if p == 0 else p - 1

    def produce(du, p):
        for part in range(2):
            cols = slice(part * chunk, (part + 1) * chunk)
            mine, *theirs = numer(du, part, p)
            own[slot(du, p), :, cols] = mine
            for dv in range(1, cores):
                core_send[du, dv - 1, p, :, cols] = theirs[dv - 1].astype(BF16)
        for dv in range(1, cores):
            core_copy(du, dv, p).start()

    def pass_on(du, p):
        value = own[slot(du, p)]
        for dv in range(1, cores):
            core_copy(du, dv, p).wait_recv()
            value += core_recv[du, dv - 1, p].astype(F32)
        if du:
            row_send[du - 1, p] = value.astype(BF16)
            if far > 1:
                row_copy(du, p, True).start()
        else:
            own[slot(0, p)] = value

    others = [(du, p) for du in range(1, outer) for p in range(steps)]
    for b in range(near):
        mass += jnp.dot(
            mass_sum[b], wide_marks[b * block : b * block + LANES, :].astype(F32),
            precision=HIGHEST, preferred_element_type=F32,
        )
    mass_part[...] = mass.reshape(mass_part.shape)
    for d in range(1, far):
        mass_far(d).start()
    for du, p in others:
        produce(du, p)
    produce(0, 0)
    for du, p in others:
        pass_on(du, p)
    for p in range(1, steps):
        produce(0, p)
    for du, p in others:
        row_copy(du, p, False).start()
    for p in range(steps):
        pass_on(0, p)
    value = mass_part[0]
    for d in range(1, far):
        mass_far(d).wait_recv()
        value += mass_recv[d]
    mass_all[0] = value
    for d in range(1, n_img):
        mass_img(d).start()

    def far_copy(d, p):
        return remote(
            core_send.at[0, 0, p, pl.ds(d * classes, classes)], far_recv.at[d, p], f3_s.at[d, p], f3_r.at[d, p], far_id(d)
        )

    for p in range(steps):
        for dv in range(1, cores):
            core_copy(0, dv, p).wait_send()
        for du in range(1, outer):
            if far > 1:
                row_copy(du, p, True).wait_recv()
        for d in range(1, far):
            part = slice(d * classes, (d + 1) * classes)
            value = own[slot(0, p), part]
            for du in range(1, outer):
                value += row_recv[du - 1, p, part].astype(F32)
            core_send[0, 0, p, part] = value.astype(BF16)
            far_copy(d, p).start()

    for d in range(1, far):
        resp_far(d).wait_recv()
    resp_recv[0] = resp_send[0]
    pair = near * rows
    total = rows * n_cls
    for t in range(-(-total // LANES)):
        value = jnp.zeros((classes, LANES), F32)
        source = lane // pair + t * (LANES // pair)
        for j in range(far):
            value = jnp.where(source == lax.rem(q + j, far), resp_recv[j], value)
        width = min(LANES, total - t * LANES)
        resp_ref[:, t * LANES : t * LANES + width] = value[:, :width]

    for p in range(steps):
        for du in range(1, outer):
            row_copy(du, p, False).wait_recv()
            own[slot(0, p), :classes] += row_recv[du - 1, p, :classes].astype(F32)

    for d in range(1, n_img):
        mass_img(d).wait_recv()
    mass = mass_all[0]
    for d in range(1, n_img):
        mass += mass_all[d]
    mine = pl.ds(freq_at(my_img, 0), part_freq)
    ctf = ctf_ref[:, mine]
    denom = jnp.dot(
        mass[:, :groups], ctf * ctf * nw_ref[:, mine], precision=HIGHEST,
        preferred_element_type=F32,
    ) + prior_precision

    for p in range(steps):
        value = own[slot(0, p), :classes]
        for d in range(1, far):
            far_copy(d, p).wait_recv()
            value += far_recv[d, p].astype(F32)
        cols = slice(p * chunk, (p + 1) * chunk)
        for part in range(2):
            avg_ref[:, part, cols] = value[:, part * chunk : (part + 1) * chunk] / denom[:, cols]

    for d in range(1, near):
        stat_near(d).wait_send()
        marks_near(d).wait_send()
        for p in range(steps):
            w_near(d, p).wait_send()
    for d in range(1, far):
        power_far(d).wait_send()
        resp_far(d).wait_send()
        mass_far(d).wait_send()
        for p in range(steps):
            cls_far(d, p).wait_send()
            far_copy(d, p).wait_send()
            for e in range(1, n_img):
                cls_forward(d, p, e, my_img).wait_send()
    for d in range(1, n_img):
        mass_img(d).wait_send()
    for p in range(steps):
        for du in range(outer):
            if du:
                for dv in range(1, cores):
                    core_copy(du, dv, p).wait_send()
                row_copy(du, p, False).wait_send()
                if far > 1:
                    row_copy(du, p, True).wait_send()


def settle_kernel(resp_from, avg_from, resp_to, avg_to):
    resp_to[...] = resp_from[...]
    avg_to[...] = avg_from[...]


def settle(resp, avg):
    vmem = pl.BlockSpec(memory_space=pltpu.VMEM)
    return pl.pallas_call(
        settle_kernel,
        out_shape=tuple(jax.ShapeDtypeStruct(x.shape, x.dtype) for x in (resp, avg)),
        in_specs=[vmem] * 2,
        out_specs=(vmem, vmem),
    )(resp, avg)


def local(n_cls, n_img, particles, classes, ctf, noise_weight, group_ids, shifts):
    rows, _, freq = particles.shape
    cls_rows = classes.shape[0]
    poses = shifts.shape[0]
    groups = ctf.shape[0]
    total = rows * n_cls
    part_freq = freq // n_img
    chunk = 384 if part_freq % 384 == 0 else LANES
    pad_groups = -(-groups // LANES) * LANES
    near = 2 if n_cls % 2 == 0 else 1
    cores = 2 if n_img % 2 == 0 else 1
    far = n_cls // near
    outer = n_img // cores
    steps = part_freq // chunk
    held = far * cls_rows
    wide = 2 * chunk
    block = poses * rows
    vmem = pl.BlockSpec(memory_space=pltpu.VMEM)
    dma = pltpu.SemaphoreType.DMA
    most = max(1, outer - 1)
    scratch = [
        ((rows, 2, freq), BF16),
        ((far, steps, n_img, cls_rows, 2, chunk), BF16),
        ((groups, freq), F32),
        ((1, freq), F32),
        ((rows, freq), F32),
        ((rows, pad_groups), F32),
        ((near, rows, pad_groups), BF16),
        ((near * block, pad_groups), BF16),
        ((poses, freq), F32),
        ((poses, freq), F32),
        ((steps, near, rows, n_img * wide), BF16),
        ((steps, near * block, n_img * wide), BF16),
        ((2 * held, n_img * chunk), BF16),
        ((2 * cls_rows, pad_groups), F32),
        ((far, cls_rows, pad_groups), F32),
        ((near * block // LANES, 2 * held, LANES), F32),
        ((held, near * block), F32),
        ((held, near * block), BF16),
        ((near, -(-2 * near // 8) * 8, LANES), F32),
        ((far, cls_rows, LANES), F32),
        ((far, cls_rows, LANES), F32),
        ((far, cls_rows, pad_groups), F32),
        ((far, cls_rows, pad_groups), F32),
        ((n_img, cls_rows, pad_groups), F32),
        ((outer, max(1, cores - 1), steps, held, wide), BF16),
        ((outer, max(1, cores - 1), steps, held, wide), BF16),
        ((most, steps, held, wide), BF16),
        ((most, steps, held, wide), BF16),
        ((far, steps, cls_rows, wide), BF16),
        ((most * steps + 1, held, wide), F32),
    ]
    sems = [(far, steps), (far, steps, n_img), (near, steps), (near,), (far,), (near,), (far,), (far,), (n_img,)]
    sems += [(outer, cores, steps), (outer, steps), (outer, steps), (far, steps)]
    resp, avg = pl.pallas_call(
        functools.partial(kernel, n_cls, n_img, near, cores, chunk),
        out_shape=(pltpu.VMEM((cls_rows, total), F32), pltpu.VMEM((cls_rows, 2, part_freq), F32)),
        in_specs=[pl.BlockSpec(memory_space=pltpu.SMEM)] * 2
        + [pl.BlockSpec(memory_space=pl.ANY)] * 4,
        out_specs=(vmem, vmem),
        scratch_shapes=[pltpu.VMEM(*s) for s in scratch]
        + [dma((3,)), dma((n_img, steps))]
        + [dma(s) for s in sems for _ in range(2)],
        compiler_params=pltpu.CompilerParams(
            collective_id=0, has_side_effects=True, vmem_limit_bytes=61 << 20
        ),
    )(
        group_ids,
        shifts.T,
        particles,
        classes,
        ctf,
        noise_weight,
    )
    resp, avg = settle(*(pltpu.with_memory_space_constraint(x, pltpu.VMEM) for x in (resp, avg)))
    return resp.T, avg


def solution(mesh):
    placed = (
        P(("groups", "img", "cls"), None, None),
        P(("groups", "cls"), None, None),
        P("groups", None),
        P("groups"),
        P(("groups", "img", "cls")),
        P("groups", None),
    )
    return jax.shard_map(
        functools.partial(local, mesh.shape["cls"], mesh.shape["img"]),
        mesh=mesh,
        in_specs=placed,
        out_specs=(P(("groups", "img"), "cls"), P(("groups", "cls"), None, "img")),
        check_vma=False,
    )
```

```python
import functools

import jax
import jax.numpy as jnp
from jax import lax
from jax.experimental import pallas as pl
from jax.experimental.pallas import tpu as pltpu
from jax.sharding import PartitionSpec as P

BOX = 128
LANES = 128
MESH = pl.DeviceIdType.MESH
HIGHEST = lax.Precision.HIGHEST
NT = (((1,), (1,)), ((), ()))
F32 = jnp.float32
BF16 = jnp.bfloat16

prior_precision = 0.02


def fill_phase_tables(shift_ref, cos_ref, sin_ref):
    poses, freq = cos_ref.shape
    step = 2.0 * jnp.pi / BOX
    lane = lax.broadcasted_iota(jnp.int32, (poses, BOX), 1)
    pose = lax.broadcasted_iota(jnp.int32, (poses, BOX), 0)
    move_x = jnp.zeros((poses, BOX), jnp.int32)
    move_y = jnp.zeros((poses, BOX), jnp.int32)
    for r in range(poses):
        move_x = jnp.where(pose == r, shift_ref[0, r], move_x)
        move_y = jnp.where(pose == r, shift_ref[1, r], move_y)
    move_x, move_y = move_x.astype(jnp.float32), move_y.astype(jnp.float32)
    angle_x = step * (move_x * (lane - BOX // 2).astype(jnp.float32))
    cos_x, sin_x = jnp.cos(angle_x), jnp.sin(angle_x)
    for row in range(freq // BOX):
        if row % BOX == 0:
            angle_y = step * (move_y * (lane + row).astype(jnp.float32))
            cos_rows, sin_rows = jnp.cos(angle_y), jnp.sin(angle_y)
        cos_y = cos_rows[:, row % BOX : row % BOX + 1]
        sin_y = sin_rows[:, row % BOX : row % BOX + 1]
        cols = slice(row * BOX, (row + 1) * BOX)
        cos_ref[:, cols] = cos_x * cos_y - sin_x * sin_y
        sin_ref[:, cols] = sin_x * cos_y + cos_x * sin_y


def kernel(
    n_cls, n_img, near, cores, chunk,
    ids_s, shift_ref, part_hbm, cls_hbm, ctf_hbm, nw_hbm,
    resp_ref, avg_ref,
    part_ref, cls_raw, ctf_ref, nw_ref, sel, onehot, marks, wide_marks, cos_ref, sin_ref,
    wbuf, turned, cls_mat, power_rows, power_buf, partial, scores, rho_low, stat, resp_send, resp_recv,
    mass_part, mass_recv, mass_all,
    core_send, core_recv, row_send, row_recv, far_recv, own,
    in_sem, cl_sem, cq_s, cq_r, cf_s, cf_r, wh_s, wh_r, mk_s, mk_r, pw_s, pw_r, st_s, st_r, rp_s, rp_r,
    m1_s, m1_r, m2_s, m2_r, c1_s, c1_r, r2_s, r2_r, o2_s, o2_r, f3_s, f3_r,
):
    rows = part_ref.shape[0]
    freq = ctf_ref.shape[1]
    groups = ctf_ref.shape[0]
    classes = cls_raw.shape[3]
    poses = cos_ref.shape[0]
    far = n_cls // near
    outer = n_img // cores
    part_freq = freq // n_img
    steps = part_freq // chunk
    wide = 2 * chunk
    block = poses * rows
    held = far * classes
    my_cls = lax.axis_index("cls")
    my_img = lax.axis_index("img")
    q, h = my_cls // near, lax.rem(my_cls, near)
    u, v = my_img // cores, lax.rem(my_img, cores)

    def near_id(d):
        return {"cls": q * near + lax.rem(h + d, near)}

    def far_id(d):
        return {"cls": lax.rem(q + d, far) * near + h}

    def img_id(d):
        return {"img": lax.rem(my_img + d, n_img)}

    def core_id(d):
        return {"img": u * cores + lax.rem(v + d, cores)}

    def outer_id(d):
        return {"img": lax.rem(u + d, outer) * cores + v}

    def remote(src, dst, send, recv, device):
        return pltpu.make_async_remote_copy(
            src_ref=src, dst_ref=dst, send_sem=send, recv_sem=recv,
            device_id=device, device_id_type=MESH,
        )

    barrier = pltpu.get_barrier_semaphore()
    peers = (
        [near_id(d) for d in range(1, near)]
        + [far_id(d) for d in range(1, far)]
        + [img_id(d) for d in range(1, n_img)]
    )
    for peer in peers:
        pl.semaphore_signal(barrier, inc=1, device_id=peer, device_id_type=MESH)

    def freq_at(img, p):
        return pl.multiple_of(img * part_freq + p * chunk, LANES)

    def cls_load(e, p):
        img = lax.rem(my_img + e, n_img)
        return pltpu.make_async_copy(
            cls_hbm.at[:, :, pl.ds(freq_at(img, p), chunk)], cls_raw.at[0, p, img], cl_sem.at[e, p]
        )

    inputs = [
        pltpu.make_async_copy(src, dst, in_sem.at[i])
        for i, (src, dst) in enumerate(
            ((ctf_hbm, ctf_ref), (nw_hbm, nw_ref.at[0]), (part_hbm, part_ref))
        )
    ]
    for p in range(steps):
        cls_load(0, p).start()
    for copy in inputs:
        copy.start()
    for e in range(1, n_img):
        for p in range(steps):
            cls_load(e, p).start()

    def cls_far(d, p):
        return remote(
            cls_raw.at[0, p, my_img], cls_raw.at[far - d, p, my_img],
            cq_s.at[d, p], cq_r.at[d, p], far_id(d),
        )

    def cls_forward(j, p, e, img):
        piece = cls_raw.at[j, p, img]
        return remote(piece, piece, cf_s.at[j, p, e], cf_r.at[j, p, e], img_id(e))

    def w_near(d, p):
        return remote(
            wbuf.at[p, 0], wbuf.at[p, near - d], wh_s.at[d, p], wh_r.at[d, p], near_id(d)
        )

    def marks_near(d):
        return remote(marks.at[0], marks.at[near - d], mk_s.at[d], mk_r.at[d], near_id(d))

    def power_far(d):
        return remote(
            power_buf.at[0], power_buf.at[far - d], pw_s.at[d], pw_r.at[d], far_id(d)
        )

    pl.semaphore_wait(barrier, len(peers))
    for p in range(steps):
        cls_load(0, p).wait()
        for d in range(1, far):
            cls_far(d, p).start()

    for copy in inputs:
        copy.wait()
    for i in range(rows):
        sel[pl.ds(i, 1), :] = ctf_ref[pl.ds(ids_s[i], 1), :] * nw_ref[...]
        onehot[pl.ds(i, 1), :] = (
            lax.broadcasted_iota(jnp.int32, (1, onehot.shape[1]), 1) == ids_s[i]
        ).astype(F32)
    for p in range(steps):
        for i in range(n_img):
            cols = slice(i * part_freq + p * chunk, i * part_freq + (p + 1) * chunk)
            for part in range(2):
                at = i * wide + part * chunk
                wbuf[p, 0, :, at : at + chunk] = (
                    part_ref[:, part, cols].astype(F32) * sel[:, cols]
                ).astype(BF16)
        for d in range(1, near):
            w_near(d, p).start()
    marks[0] = onehot[...].astype(BF16)
    for d in range(1, near):
        marks_near(d).start()

    fill_phase_tables(shift_ref, cos_ref, sin_ref)

    half = n_img * chunk

    def turn(p, b):
        def one(i, carry):
            at = pl.ds(freq_at(i, p), chunk)
            re_from = pl.ds(pl.multiple_of(i * wide, LANES), chunk)
            im_from = pl.ds(pl.multiple_of(i * wide + chunk, LANES), chunk)
            re_at = pl.ds(pl.multiple_of(i * chunk, LANES), chunk)
            im_at = pl.ds(pl.multiple_of(half + i * chunk, LANES), chunk)
            re = wbuf[p, b, :, re_from].astype(F32)
            im = wbuf[p, b, :, im_from].astype(F32)
            for r in range(poses):
                cos_r = cos_ref[r : r + 1, at]
                sin_r = sin_ref[r : r + 1, at]
                out = slice(b * block + r * rows, b * block + (r + 1) * rows)
                turned[p, out, re_at] = (re * cos_r + im * sin_r).astype(BF16)
                turned[p, out, im_at] = (im * cos_r - re * sin_r).astype(BF16)
            return carry

        lax.fori_loop(0, n_img, one, 0)

    by_distance = sorted(range(1, n_img), key=lambda e: e % cores == 0, reverse=True)

    def relay(p):
        for d in range(1, far):
            cls_far(d, p).wait_recv()
            for e in by_distance:
                cls_forward(far - d, p, e, my_img).start()

    for p in range(steps):
        turn(p, 0)
        if p == min(1, steps - 1):
            relay(0)
    for e in range(1, n_img):
        for p in range(steps):
            cls_load(e, p).wait()

    def halves(x):
        top = x.astype(BF16)
        return jnp.concatenate([top, (x - top.astype(F32)).astype(BF16)], axis=0)

    def power_step(p, total):
        for i in range(n_img):
            at = pl.ds(freq_at(i, p), chunk)
            value = cls_raw[0, p, i].reshape(2 * classes, chunk).astype(F32)
            ctf = ctf_ref[:, at]
            total += lax.dot_general(
                halves(value * value), halves(ctf * ctf * nw_ref[:, at]), NT,
                preferred_element_type=F32,
            )
        return total

    if steps > 1:
        relay(1)
    power = lax.fori_loop(0, steps, power_step, jnp.zeros((4 * classes, 2 * groups), F32))
    power_rows[...] = jnp.zeros_like(power_rows)
    power_rows[:, :groups] = (
        power[: 2 * classes, :groups] + power[: 2 * classes, groups:] + power[2 * classes :, :groups]
    )
    power_buf[0] = (
        power_rows[pl.ds(0, classes, stride=2), :] + power_rows[pl.ds(1, classes, stride=2), :]
    )
    for d in range(1, far):
        power_far(d).start()
    def turn_near(p):
        for d in range(1, near):
            w_near(d, p).wait_recv()
            turn(p, near - d)

    turn_near(0)
    if steps > 2:
        relay(2)

    tiles = block // LANES

    def match(p, b):
        row = lax.broadcasted_iota(jnp.int32, (2 * held, block), 0)
        pair = [
            lax.dot_general(
                cls_mat[...],
                turned[p, b * block : (b + 1) * block, part * half : (part + 1) * half],
                NT,
                preferred_element_type=F32,
            )
            for part in range(2)
        ]
        value = jnp.where(row % 2 == 0, pair[0], pair[1])
        for t in range(tiles):
            at = slice(t * LANES, (t + 1) * LANES)
            if p:
                partial[b * tiles + t] += value[:, at]
            else:
                partial[b * tiles + t] = value[:, at]

    def match_all(p):
        for j in range(1, far):
            for e in range(1, n_img):
                cls_forward(j, p, e, lax.rem(my_img + n_img - e, n_img)).wait_recv()

        def lay(i, carry):
            at = pl.ds(pl.multiple_of(i * chunk, LANES), chunk)
            for j in range(far):
                cls_mat[2 * j * classes : 2 * (j + 1) * classes, at] = cls_raw[j, p, i].reshape(
                    2 * classes, chunk
                )
            return carry

        lax.fori_loop(0, n_img, lay, 0)
        for b in range(near):
            match(p, b)

    def penalise():
        for d in range(1, near):
            marks_near(d).wait_recv()
        for b in range(near):
            for r in range(poses):
                wide_marks[b * block + r * rows : b * block + (r + 1) * rows, :] = marks[b]
        for d in range(1, far):
            power_far(d).wait_recv()
        rest = -0.5 * power_buf[...].reshape(held, power_buf.shape[2])
        penalty = jnp.zeros(scores.shape, F32)
        for _ in range(3):
            top = rest.astype(BF16)
            rest = rest - top.astype(F32)
            penalty += lax.dot_general(top, wide_marks[...], NT, preferred_element_type=F32)
        scores[...] = penalty

    for p in range(steps):
        if p:
            turn_near(p)
        if p == steps - 1:
            penalise()
        if p > 2:
            relay(p)
        match_all(p)

    for k in range(near * tiles):
        at = slice(k * LANES, (k + 1) * LANES)
        scores[:, at] += (
            partial[k, pl.ds(0, held, stride=2), :] + partial[k, pl.ds(1, held, stride=2), :]
        )


    def over_poses(op, pieces):
        value = functools.reduce(op, pieces)
        shift = LANES // 2
        while shift >= rows:
            value = op(value, pltpu.roll(value, shift, 1))
            shift //= 2
        return value

    def tile(b, t):
        return slice(b * block + t * LANES, b * block + (t + 1) * LANES)

    pose_peak, pose_sum, peak, mass_sum = [], [], [], []
    for b in range(near):
        top = over_poses(jnp.maximum, [scores[:, tile(b, t)] for t in range(tiles)])
        total = over_poses(jnp.add, [jnp.exp(scores[:, tile(b, t)] - top) for t in range(tiles)])
        whole = jnp.max(top, axis=0, keepdims=True)
        pose_peak.append(top)
        pose_sum.append(total)
        peak.append(whole)
        mass_sum.append(jnp.sum(total * jnp.exp(top - whole), axis=0, keepdims=True))
        stat[0, b : b + 1, :] = whole
        stat[0, near + b : near + b + 1, :] = mass_sum[b]

    def stat_near(d):
        return remote(stat.at[0], stat.at[d], st_s.at[d], st_r.at[d], near_id(d))

    for d in range(1, near):
        stat_near(d).start()
    log_sums = [pose_peak[b] + jnp.log(pose_sum[b]) for b in range(near)]
    for d in range(1, near):
        stat_near(d).wait_recv()
    mass = jnp.zeros((held, marks.shape[2]), F32)
    lane = lax.broadcasted_iota(jnp.int32, (1, LANES), 1)
    lane_h = lax.rem(lane // rows, near)
    both = jnp.zeros((held, LANES), F32)
    for b in range(near):
        tops = [stat[d, (b + d) % near : (b + d) % near + 1, :] for d in range(near)]
        sums = [stat[d, near + (b + d) % near : near + (b + d) % near + 1, :] for d in range(near)]
        whole = functools.reduce(jnp.maximum, tops)
        norm = functools.reduce(jnp.add, [s * jnp.exp(t - whole) for s, t in zip(sums, tops)])
        log_norm = whole + jnp.log(norm)
        for t in range(tiles):
            rho_low[:, tile(b, t)] = jnp.exp(scores[:, tile(b, t)] - log_norm).astype(BF16)
        pose_total = pose_sum[b] * jnp.exp(pose_peak[b] - log_norm)
        mass_sum[b] = jnp.where(lane < rows, pose_total, 0.0)
        both = jnp.where(lane_h == lax.rem(h + b, near), log_sums[b] - log_norm, both)
    resp_send[...] = both.reshape(resp_send.shape)

    def resp_far(d):
        return remote(resp_send.at[d], resp_recv.at[far - d], rp_s.at[d], rp_r.at[d], far_id(d))

    for d in range(1, far):
        resp_far(d).start()

    def numer(du, part, p):
        width = cores * chunk
        at = pl.multiple_of(part * half + lax.rem(u + du, outer) * width, LANES)
        value = jnp.dot(
            rho_low[...], turned[p, :, pl.ds(at, width)], preferred_element_type=F32
        )
        pieces = [value[:, c * chunk : (c + 1) * chunk] for c in range(cores)]

        def piece(dv):
            chosen = pieces[0]
            for c in range(1, cores):
                chosen = jnp.where(lax.rem(v + dv, cores) == c, pieces[c], chosen)
            return chosen

        return [piece(dv) for dv in range(cores)]

    def core_copy(du, dv, p):
        return remote(
            core_send.at[du, dv - 1, p], core_recv.at[du, dv - 1, p],
            c1_s.at[du, dv, p], c1_r.at[du, dv, p], core_id(dv),
        )

    def row_copy(du, p, theirs):
        part = pl.ds(classes, held - classes) if theirs else pl.ds(0, classes)
        send, recv = (r2_s, r2_r) if theirs else (o2_s, o2_r)
        return remote(
            row_send.at[du - 1, p, part], row_recv.at[du - 1, p, part],
            send.at[du, p], recv.at[du, p], outer_id(du),
        )

    def mass_far(d):
        return remote(
            mass_part.at[d], mass_recv.at[d], m1_s.at[d], m1_r.at[d], far_id(d)
        )

    def mass_img(d):
        return remote(mass_all.at[0], mass_all.at[d], m2_s.at[d], m2_r.at[d], img_id(d))

    def slot(du, p):
        if du:
            return (du - 1) * steps + p
        return max(1, outer - 1) * steps if p == 0 else p - 1

    def produce(du, p):
        for part in range(2):
            cols = slice(part * chunk, (part + 1) * chunk)
            mine, *theirs = numer(du, part, p)
            own[slot(du, p), :, cols] = mine
            for dv in range(1, cores):
                core_send[du, dv - 1, p, :, cols] = theirs[dv - 1].astype(BF16)
        for dv in range(1, cores):
            core_copy(du, dv, p).start()

    def pass_on(du, p):
        value = own[slot(du, p)]
        for dv in range(1, cores):
            core_copy(du, dv, p).wait_recv()
            value += core_recv[du, dv - 1, p].astype(F32)
        if du:
            row_send[du - 1, p] = value.astype(BF16)
            if far > 1:
                row_copy(du, p, True).start()
        else:
            own[slot(0, p)] = value

    others = [(du, p) for du in range(1, outer) for p in range(steps)]
    for b in range(near):
        mass += jnp.dot(
            mass_sum[b], wide_marks[b * block : b * block + LANES, :].astype(F32),
            precision=HIGHEST, preferred_element_type=F32,
        )
    mass_part[...] = mass.reshape(mass_part.shape)
    for d in range(1, far):
        mass_far(d).start()
    for du, p in others:
        produce(du, p)
    produce(0, 0)
    for du, p in others:
        pass_on(du, p)
    for p in range(1, steps):
        produce(0, p)
    for du, p in others:
        row_copy(du, p, False).start()
    value = mass_part[0]
    for d in range(1, far):
        mass_far(d).wait_recv()
        value += mass_recv[d]
    mass_all[0] = value
    for d in range(1, n_img):
        mass_img(d).start()

    def far_copy(d, p):
        return remote(
            core_send.at[0, 0, p, pl.ds(d * classes, classes)], far_recv.at[d, p], f3_s.at[d, p], f3_r.at[d, p], far_id(d)
        )

    for p in range(steps):
        pass_on(0, p)
        for dv in range(1, cores):
            core_copy(0, dv, p).wait_send()
        for du in range(1, outer):
            if far > 1:
                row_copy(du, p, True).wait_recv()
        for d in range(1, far):
            part = slice(d * classes, (d + 1) * classes)
            value = own[slot(0, p), part]
            for du in range(1, outer):
                value += row_recv[du - 1, p, part].astype(F32)
            core_send[0, 0, p, part] = value.astype(BF16)
            far_copy(d, p).start()

    for d in range(1, far):
        resp_far(d).wait_recv()
    resp_recv[0] = resp_send[0]
    pair = near * rows
    total = rows * n_cls
    for t in range(-(-total // LANES)):
        value = jnp.zeros((classes, LANES), F32)
        source = lane // pair + t * (LANES // pair)
        for j in range(far):
            value = jnp.where(source == lax.rem(q + j, far), resp_recv[j], value)
        width = min(LANES, total - t * LANES)
        resp_ref[:, t * LANES : t * LANES + width] = value[:, :width]

    for p in range(steps):
        for du in range(1, outer):
            row_copy(du, p, False).wait_recv()
            own[slot(0, p), :classes] += row_recv[du - 1, p, :classes].astype(F32)

    for d in range(1, n_img):
        mass_img(d).wait_recv()
    mass = mass_all[0]
    for d in range(1, n_img):
        mass += mass_all[d]
    mine = pl.ds(freq_at(my_img, 0), part_freq)
    ctf = ctf_ref[:, mine]
    denom = jnp.dot(
        mass[:, :groups], ctf * ctf * nw_ref[:, mine], precision=HIGHEST,
        preferred_element_type=F32,
    ) + prior_precision
    scale = 1.0 / denom

    for d in range(1, near):
        stat_near(d).wait_send()
        marks_near(d).wait_send()
        for p in range(steps):
            w_near(d, p).wait_send()
    for d in range(1, far):
        power_far(d).wait_send()
        resp_far(d).wait_send()
        mass_far(d).wait_send()
        for p in range(steps):
            cls_far(d, p).wait_send()
            for e in range(1, n_img):
                cls_forward(d, p, e, my_img).wait_send()
    for p in range(steps):
        for du in range(outer):
            if du:
                for dv in range(1, cores):
                    core_copy(du, dv, p).wait_send()
                row_copy(du, p, False).wait_send()
                if far > 1:
                    row_copy(du, p, True).wait_send()

    for p in range(steps):
        value = own[slot(0, p), :classes]
        for d in range(1, far):
            far_copy(d, p).wait_recv()
            value += far_recv[d, p].astype(F32)
        cols = slice(p * chunk, (p + 1) * chunk)
        for part in range(2):
            avg_ref[:, part, cols] = value[:, part * chunk : (part + 1) * chunk] * scale[:, cols]

    for d in range(1, far):
        for p in range(steps):
            far_copy(d, p).wait_send()
    for d in range(1, n_img):
        mass_img(d).wait_send()


def settle_kernel(resp_from, avg_from, resp_to, avg_to):
    resp_to[...] = resp_from[...]
    avg_to[...] = avg_from[...]


def settle(resp, avg):
    vmem = pl.BlockSpec(memory_space=pltpu.VMEM)
    return pl.pallas_call(
        settle_kernel,
        out_shape=tuple(jax.ShapeDtypeStruct(x.shape, x.dtype) for x in (resp, avg)),
        in_specs=[vmem] * 2,
        out_specs=(vmem, vmem),
    )(resp, avg)


def local(n_cls, n_img, particles, classes, ctf, noise_weight, group_ids, shifts):
    rows, _, freq = particles.shape
    cls_rows = classes.shape[0]
    poses = shifts.shape[0]
    groups = ctf.shape[0]
    total = rows * n_cls
    part_freq = freq // n_img
    chunk = 384 if part_freq % 384 == 0 else LANES
    pad_groups = -(-groups // LANES) * LANES
    near = 2 if n_cls % 2 == 0 else 1
    cores = 2 if n_img % 2 == 0 else 1
    far = n_cls // near
    outer = n_img // cores
    steps = part_freq // chunk
    held = far * cls_rows
    wide = 2 * chunk
    block = poses * rows
    vmem = pl.BlockSpec(memory_space=pltpu.VMEM)
    dma = pltpu.SemaphoreType.DMA
    most = max(1, outer - 1)
    scratch = [
        ((rows, 2, freq), BF16),
        ((far, steps, n_img, cls_rows, 2, chunk), BF16),
        ((groups, freq), F32),
        ((1, freq), F32),
        ((rows, freq), F32),
        ((rows, pad_groups), F32),
        ((near, rows, pad_groups), BF16),
        ((near * block, pad_groups), BF16),
        ((poses, freq), F32),
        ((poses, freq), F32),
        ((steps, near, rows, n_img * wide), BF16),
        ((steps, near * block, n_img * wide), BF16),
        ((2 * held, n_img * chunk), BF16),
        ((2 * cls_rows, pad_groups), F32),
        ((far, cls_rows, pad_groups), F32),
        ((near * block // LANES, 2 * held, LANES), F32),
        ((held, near * block), F32),
        ((held, near * block), BF16),
        ((near, -(-2 * near // 8) * 8, LANES), F32),
        ((far, cls_rows, LANES), F32),
        ((far, cls_rows, LANES), F32),
        ((far, cls_rows, pad_groups), F32),
        ((far, cls_rows, pad_groups), F32),
        ((n_img, cls_rows, pad_groups), F32),
        ((outer, max(1, cores - 1), steps, held, wide), BF16),
        ((outer, max(1, cores - 1), steps, held, wide), BF16),
        ((most, steps, held, wide), BF16),
        ((most, steps, held, wide), BF16),
        ((far, steps, cls_rows, wide), BF16),
        ((most * steps + 1, held, wide), F32),
    ]
    sems = [(far, steps), (far, steps, n_img), (near, steps), (near,), (far,), (near,), (far,), (far,), (n_img,)]
    sems += [(outer, cores, steps), (outer, steps), (outer, steps), (far, steps)]
    resp, avg = pl.pallas_call(
        functools.partial(kernel, n_cls, n_img, near, cores, chunk),
        out_shape=(pltpu.VMEM((cls_rows, total), F32), pltpu.VMEM((cls_rows, 2, part_freq), F32)),
        in_specs=[pl.BlockSpec(memory_space=pltpu.SMEM)] * 2
        + [pl.BlockSpec(memory_space=pl.ANY)] * 4,
        out_specs=(vmem, vmem),
        scratch_shapes=[pltpu.VMEM(*s) for s in scratch]
        + [dma((3,)), dma((n_img, steps))]
        + [dma(s) for s in sems for _ in range(2)],
        compiler_params=pltpu.CompilerParams(
            collective_id=0, has_side_effects=True, vmem_limit_bytes=61 << 20
        ),
    )(
        group_ids,
        shifts.T,
        particles,
        classes,
        ctf,
        noise_weight,
    )
    resp, avg = settle(*(pltpu.with_memory_space_constraint(x, pltpu.VMEM) for x in (resp, avg)))
    return resp.T, avg


def solution(mesh):
    placed = (
        P(("groups", "img", "cls"), None, None),
        P(("groups", "cls"), None, None),
        P("groups", None),
        P("groups"),
        P(("groups", "img", "cls")),
        P("groups", None),
    )
    return jax.shard_map(
        functools.partial(local, mesh.shape["cls"], mesh.shape["img"]),
        mesh=mesh,
        in_specs=placed,
        out_specs=(P(("groups", "img"), "cls"), P(("groups", "cls"), None, "img")),
        check_vma=False,
    )
```

```python
import functools

import jax
import jax.numpy as jnp
from jax import lax
from jax.experimental import pallas as pl
from jax.experimental.pallas import tpu as pltpu
from jax.sharding import PartitionSpec as P

BOX = 128
LANES = 128
MESH = pl.DeviceIdType.MESH
HIGHEST = lax.Precision.HIGHEST
NT = (((1,), (1,)), ((), ()))
F32 = jnp.float32
BF16 = jnp.bfloat16

prior_precision = 0.02


def fill_phase_tables(shift_ref, cos_ref, sin_ref):
    poses, freq = cos_ref.shape
    step = 2.0 * jnp.pi / BOX
    lane = lax.broadcasted_iota(jnp.int32, (poses, BOX), 1)
    pose = lax.broadcasted_iota(jnp.int32, (poses, BOX), 0)
    move_x = jnp.zeros((poses, BOX), jnp.int32)
    move_y = jnp.zeros((poses, BOX), jnp.int32)
    for r in range(poses):
        move_x = jnp.where(pose == r, shift_ref[0, r], move_x)
        move_y = jnp.where(pose == r, shift_ref[1, r], move_y)
    move_x, move_y = move_x.astype(jnp.float32), move_y.astype(jnp.float32)
    angle_x = step * (move_x * (lane - BOX // 2).astype(jnp.float32))
    cos_x, sin_x = jnp.cos(angle_x), jnp.sin(angle_x)
    for row in range(freq // BOX):
        if row % BOX == 0:
            angle_y = step * (move_y * (lane + row).astype(jnp.float32))
            cos_rows, sin_rows = jnp.cos(angle_y), jnp.sin(angle_y)
        cos_y = cos_rows[:, row % BOX : row % BOX + 1]
        sin_y = sin_rows[:, row % BOX : row % BOX + 1]
        cols = slice(row * BOX, (row + 1) * BOX)
        cos_ref[:, cols] = cos_x * cos_y - sin_x * sin_y
        sin_ref[:, cols] = sin_x * cos_y + cos_x * sin_y


def kernel(
    n_cls, n_img, near, cores, chunk,
    ids_s, shift_ref, part_hbm, cls_hbm, ctf_hbm, nw_hbm,
    resp_ref, avg_ref,
    part_ref, cls_raw, ctf_ref, nw_ref, sel, onehot, marks, wide_marks, cos_ref, sin_ref,
    wbuf, turned, cls_mat, power_rows, power_buf, partial, scores, rho_low, stat, resp_send, resp_recv,
    mass_part, mass_recv, mass_all,
    core_send, core_recv, row_send, row_recv, far_recv, own,
    in_sem, cl_sem, cq_s, cq_r, cf_s, cf_r, wh_s, wh_r, mk_s, mk_r, pw_s, pw_r, st_s, st_r, rp_s, rp_r,
    m1_s, m1_r, m2_s, m2_r, c1_s, c1_r, r2_s, r2_r, o2_s, o2_r, f3_s, f3_r,
):
    rows = part_ref.shape[0]
    freq = ctf_ref.shape[1]
    groups = ctf_ref.shape[0]
    classes = cls_raw.shape[3]
    poses = cos_ref.shape[0]
    far = n_cls // near
    outer = n_img // cores
    part_freq = freq // n_img
    steps = part_freq // chunk
    wide = 2 * chunk
    block = poses * rows
    held = far * classes
    my_cls = lax.axis_index("cls")
    my_img = lax.axis_index("img")
    q, h = my_cls // near, lax.rem(my_cls, near)
    u, v = my_img // cores, lax.rem(my_img, cores)

    def near_id(d):
        return {"cls": q * near + lax.rem(h + d, near)}

    def far_id(d):
        return {"cls": lax.rem(q + d, far) * near + h}

    def img_id(d):
        return {"img": lax.rem(my_img + d, n_img)}

    def core_id(d):
        return {"img": u * cores + lax.rem(v + d, cores)}

    def outer_id(d):
        return {"img": lax.rem(u + d, outer) * cores + v}

    def remote(src, dst, send, recv, device):
        return pltpu.make_async_remote_copy(
            src_ref=src, dst_ref=dst, send_sem=send, recv_sem=recv,
            device_id=device, device_id_type=MESH,
        )

    barrier = pltpu.get_barrier_semaphore()
    peers = (
        [near_id(d) for d in range(1, near)]
        + [far_id(d) for d in range(1, far)]
        + [img_id(d) for d in range(1, n_img)]
    )
    for peer in peers:
        pl.semaphore_signal(barrier, inc=1, device_id=peer, device_id_type=MESH)

    def freq_at(img, p):
        return pl.multiple_of(img * part_freq + p * chunk, LANES)

    def cls_load(e, p):
        img = lax.rem(my_img + e, n_img)
        return pltpu.make_async_copy(
            cls_hbm.at[:, :, pl.ds(freq_at(img, p), chunk)], cls_raw.at[0, p, img], cl_sem.at[e, p]
        )

    inputs = [
        pltpu.make_async_copy(src, dst, in_sem.at[i])
        for i, (src, dst) in enumerate(
            ((ctf_hbm, ctf_ref), (nw_hbm, nw_ref.at[0]), (part_hbm, part_ref))
        )
    ]
    for p in range(steps):
        cls_load(0, p).start()
    for copy in inputs:
        copy.start()
    for e in range(1, n_img):
        for p in range(steps):
            cls_load(e, p).start()

    def cls_far(d, p):
        return remote(
            cls_raw.at[0, p, my_img], cls_raw.at[far - d, p, my_img],
            cq_s.at[d, p], cq_r.at[d, p], far_id(d),
        )

    def cls_forward(j, p, e, img):
        piece = cls_raw.at[j, p, img]
        return remote(piece, piece, cf_s.at[j, p, e], cf_r.at[j, p, e], img_id(e))

    def w_near(d, p):
        return remote(
            wbuf.at[p, 0], wbuf.at[p, near - d], wh_s.at[d, p], wh_r.at[d, p], near_id(d)
        )

    def marks_near(d):
        return remote(marks.at[0], marks.at[near - d], mk_s.at[d], mk_r.at[d], near_id(d))

    def power_far(d):
        return remote(
            power_buf.at[0], power_buf.at[far - d], pw_s.at[d], pw_r.at[d], far_id(d)
        )

    pl.semaphore_wait(barrier, len(peers))
    for p in range(steps):
        cls_load(0, p).wait()
        for d in range(1, far):
            cls_far(d, p).start()

    for copy in inputs:
        copy.wait()
    for i in range(rows):
        sel[pl.ds(i, 1), :] = ctf_ref[pl.ds(ids_s[i], 1), :] * nw_ref[...]
        onehot[pl.ds(i, 1), :] = (
            lax.broadcasted_iota(jnp.int32, (1, onehot.shape[1]), 1) == ids_s[i]
        ).astype(F32)
    for p in range(steps):
        for i in range(n_img):
            cols = slice(i * part_freq + p * chunk, i * part_freq + (p + 1) * chunk)
            for part in range(2):
                at = i * wide + part * chunk
                wbuf[p, 0, :, at : at + chunk] = (
                    part_ref[:, part, cols].astype(F32) * sel[:, cols]
                ).astype(BF16)
        for d in range(1, near):
            w_near(d, p).start()
    marks[0] = onehot[...].astype(BF16)
    for d in range(1, near):
        marks_near(d).start()

    fill_phase_tables(shift_ref, cos_ref, sin_ref)

    half = n_img * chunk

    def turn(p, b):
        def one(i, carry):
            at = pl.ds(freq_at(i, p), chunk)
            re_from = pl.ds(pl.multiple_of(i * wide, LANES), chunk)
            im_from = pl.ds(pl.multiple_of(i * wide + chunk, LANES), chunk)
            re_at = pl.ds(pl.multiple_of(i * chunk, LANES), chunk)
            im_at = pl.ds(pl.multiple_of(half + i * chunk, LANES), chunk)
            re = wbuf[p, b, :, re_from].astype(F32)
            im = wbuf[p, b, :, im_from].astype(F32)
            for r in range(poses):
                cos_r = cos_ref[r : r + 1, at]
                sin_r = sin_ref[r : r + 1, at]
                out = slice(b * block + r * rows, b * block + (r + 1) * rows)
                turned[p, out, re_at] = (re * cos_r + im * sin_r).astype(BF16)
                turned[p, out, im_at] = (im * cos_r - re * sin_r).astype(BF16)
            return carry

        lax.fori_loop(0, n_img, one, 0)

    by_distance = sorted(range(1, n_img), key=lambda e: e % cores == 0, reverse=True)

    def relay(p):
        for d in range(1, far):
            cls_far(d, p).wait_recv()
            for e in by_distance:
                cls_forward(far - d, p, e, my_img).start()

    for p in range(steps):
        turn(p, 0)
        if p == min(1, steps - 1):
            relay(0)
    for e in range(1, n_img):
        for p in range(steps):
            cls_load(e, p).wait()

    def halves(x):
        top = x.astype(BF16)
        return jnp.concatenate([top, (x - top.astype(F32)).astype(BF16)], axis=0)

    def power_step(p, total):
        for i in range(n_img):
            at = pl.ds(freq_at(i, p), chunk)
            value = cls_raw[0, p, i].reshape(2 * classes, chunk).astype(F32)
            ctf = ctf_ref[:, at]
            total += lax.dot_general(
                halves(value * value), halves(ctf * ctf * nw_ref[:, at]), NT,
                preferred_element_type=F32,
            )
        return total

    if steps > 1:
        relay(1)
    power = lax.fori_loop(0, steps, power_step, jnp.zeros((4 * classes, 2 * groups), F32))
    power_rows[...] = jnp.zeros_like(power_rows)
    power_rows[:, :groups] = (
        power[: 2 * classes, :groups] + power[: 2 * classes, groups:] + power[2 * classes :, :groups]
    )
    power_buf[0] = (
        power_rows[pl.ds(0, classes, stride=2), :] + power_rows[pl.ds(1, classes, stride=2), :]
    )
    for d in range(1, far):
        power_far(d).start()
    def turn_near(p):
        for d in range(1, near):
            w_near(d, p).wait_recv()
            turn(p, near - d)

    turn_near(0)
    if steps > 2:
        relay(2)

    tiles = block // LANES

    def match(p, b):
        row = lax.broadcasted_iota(jnp.int32, (2 * held, block), 0)
        pair = [
            lax.dot_general(
                cls_mat[...],
                turned[p, b * block : (b + 1) * block, part * half : (part + 1) * half],
                NT,
                preferred_element_type=F32,
            )
            for part in range(2)
        ]
        value = jnp.where(row % 2 == 0, pair[0], pair[1])
        for t in range(tiles):
            at = slice(t * LANES, (t + 1) * LANES)
            if p:
                partial[b * tiles + t] += value[:, at]
            else:
                partial[b * tiles + t] = value[:, at]

    def match_all(p):
        for j in range(1, far):
            for e in range(1, n_img):
                cls_forward(j, p, e, lax.rem(my_img + n_img - e, n_img)).wait_recv()

        def lay(i, carry):
            at = pl.ds(pl.multiple_of(i * chunk, LANES), chunk)
            for j in range(far):
                cls_mat[2 * j * classes : 2 * (j + 1) * classes, at] = cls_raw[j, p, i].reshape(
                    2 * classes, chunk
                )
            return carry

        lax.fori_loop(0, n_img, lay, 0)
        for b in range(near):
            match(p, b)

    def penalise():
        for d in range(1, near):
            marks_near(d).wait_recv()
        for b in range(near):
            for r in range(poses):
                wide_marks[b * block + r * rows : b * block + (r + 1) * rows, :] = marks[b]
        for d in range(1, far):
            power_far(d).wait_recv()
        rest = -0.5 * power_buf[...].reshape(held, power_buf.shape[2])
        penalty = jnp.zeros(scores.shape, F32)
        for _ in range(3):
            top = rest.astype(BF16)
            rest = rest - top.astype(F32)
            penalty += lax.dot_general(top, wide_marks[...], NT, preferred_element_type=F32)
        scores[...] = penalty

    for p in range(steps):
        if p == steps - 1:
            penalise()
        if p:
            turn_near(p)
        if p > 2:
            relay(p)
        match_all(p)

    for k in range(near * tiles):
        at = slice(k * LANES, (k + 1) * LANES)
        scores[:, at] += (
            partial[k, pl.ds(0, held, stride=2), :] + partial[k, pl.ds(1, held, stride=2), :]
        )


    def over_poses(op, pieces):
        value = functools.reduce(op, pieces)
        shift = LANES // 2
        while shift >= rows:
            value = op(value, pltpu.roll(value, shift, 1))
            shift //= 2
        return value

    def tile(b, t):
        return slice(b * block + t * LANES, b * block + (t + 1) * LANES)

    pose_peak, pose_sum, peak, mass_sum = [], [], [], []
    for b in range(near):
        top = over_poses(jnp.maximum, [scores[:, tile(b, t)] for t in range(tiles)])
        total = over_poses(jnp.add, [jnp.exp(scores[:, tile(b, t)] - top) for t in range(tiles)])
        whole = jnp.max(top, axis=0, keepdims=True)
        pose_peak.append(top)
        pose_sum.append(total)
        peak.append(whole)
        mass_sum.append(jnp.sum(total * jnp.exp(top - whole), axis=0, keepdims=True))
        stat[0, b : b + 1, :] = whole
        stat[0, near + b : near + b + 1, :] = mass_sum[b]

    def stat_near(d):
        return remote(stat.at[0], stat.at[d], st_s.at[d], st_r.at[d], near_id(d))

    for d in range(1, near):
        stat_near(d).start()
    log_sums = [pose_peak[b] + jnp.log(pose_sum[b]) for b in range(near)]
    for d in range(1, near):
        stat_near(d).wait_recv()
    lane = lax.broadcasted_iota(jnp.int32, (1, LANES), 1)
    lane_h = lax.rem(lane // rows, near)
    both = jnp.zeros((held, LANES), F32)
    for b in range(near):
        tops = [stat[d, (b + d) % near : (b + d) % near + 1, :] for d in range(near)]
        sums = [stat[d, near + (b + d) % near : near + (b + d) % near + 1, :] for d in range(near)]
        whole = functools.reduce(jnp.maximum, tops)
        norm = functools.reduce(jnp.add, [s * jnp.exp(t - whole) for s, t in zip(sums, tops)])
        log_norm = whole + jnp.log(norm)
        for t in range(tiles):
            rho_low[:, tile(b, t)] = jnp.exp(scores[:, tile(b, t)] - log_norm).astype(BF16)
        pose_total = pose_sum[b] * jnp.exp(pose_peak[b] - log_norm)
        mass_sum[b] = jnp.where(lane < rows, pose_total, 0.0)
        both = jnp.where(lane_h == lax.rem(h + b, near), log_sums[b] - log_norm, both)
    resp_send[...] = both.reshape(resp_send.shape)

    def resp_far(d):
        return remote(resp_send.at[d], resp_recv.at[far - d], rp_s.at[d], rp_r.at[d], far_id(d))

    for d in range(1, far):
        resp_far(d).start()

    def numer(du, part, p):
        width = cores * chunk
        at = pl.multiple_of(part * half + lax.rem(u + du, outer) * width, LANES)
        value = jnp.dot(
            rho_low[...], turned[p, :, pl.ds(at, width)], preferred_element_type=F32
        )
        pieces = [value[:, c * chunk : (c + 1) * chunk] for c in range(cores)]

        def piece(dv):
            chosen = pieces[0]
            for c in range(1, cores):
                chosen = jnp.where(lax.rem(v + dv, cores) == c, pieces[c], chosen)
            return chosen

        return [piece(dv) for dv in range(cores)]

    def core_copy(du, dv, p):
        return remote(
            core_send.at[du, dv - 1, p], core_recv.at[du, dv - 1, p],
            c1_s.at[du, dv, p], c1_r.at[du, dv, p], core_id(dv),
        )

    def row_copy(du, p, theirs):
        part = pl.ds(classes, held - classes) if theirs else pl.ds(0, classes)
        send, recv = (r2_s, r2_r) if theirs else (o2_s, o2_r)
        return remote(
            row_send.at[du - 1, p, part], row_recv.at[du - 1, p, part],
            send.at[du, p], recv.at[du, p], outer_id(du),
        )

    def mass_far(d):
        return remote(
            mass_part.at[d], mass_recv.at[d], m1_s.at[d], m1_r.at[d], far_id(d)
        )

    def mass_img(d):
        return remote(mass_all.at[0], mass_all.at[d], m2_s.at[d], m2_r.at[d], img_id(d))

    def slot(du, p):
        if du:
            return (du - 1) * steps + p
        return max(1, outer - 1) * steps if p == 0 else p - 1

    def produce(du, p):
        for part in range(2):
            cols = slice(part * chunk, (part + 1) * chunk)
            mine, *theirs = numer(du, part, p)
            own[slot(du, p), :, cols] = mine
            for dv in range(1, cores):
                core_send[du, dv - 1, p, :, cols] = theirs[dv - 1].astype(BF16)
        for dv in range(1, cores):
            core_copy(du, dv, p).start()

    def pass_on(du, p):
        value = own[slot(du, p)]
        for dv in range(1, cores):
            core_copy(du, dv, p).wait_recv()
            value += core_recv[du, dv - 1, p].astype(F32)
        if du:
            row_send[du - 1, p] = value.astype(BF16)
            if far > 1:
                row_copy(du, p, True).start()
        else:
            own[slot(0, p)] = value

    others = [(du, p) for du in range(1, outer) for p in range(steps)]
    rest, parts = jnp.concatenate(mass_sum, axis=1), []
    for _ in range(3):
        top = rest.astype(BF16)
        rest = rest - top.astype(F32)
        parts.append(top)
    split = jnp.dot(
        jnp.concatenate(parts, axis=0),
        jnp.concatenate([wide_marks[b * block : b * block + LANES, :] for b in range(near)], axis=0),
        preferred_element_type=F32,
    )
    mass = split[:held] + split[held : 2 * held] + split[2 * held :]
    mass_part[...] = mass.reshape(mass_part.shape)
    for d in range(1, far):
        mass_far(d).start()
    for du, p in others:
        produce(du, p)
    produce(0, 0)
    for du, p in others:
        pass_on(du, p)
    for p in range(1, steps):
        produce(0, p)
    for du, p in others:
        row_copy(du, p, False).start()
    value = mass_part[0]
    for d in range(1, far):
        mass_far(d).wait_recv()
        value += mass_recv[d]
    mass_all[0] = value
    for d in range(1, n_img):
        mass_img(d).start()

    def far_copy(d, p):
        return remote(
            core_send.at[0, 0, p, pl.ds(d * classes, classes)], far_recv.at[d, p], f3_s.at[d, p], f3_r.at[d, p], far_id(d)
        )

    for p in range(steps):
        pass_on(0, p)
        for dv in range(1, cores):
            core_copy(0, dv, p).wait_send()
        for du in range(1, outer):
            if far > 1:
                row_copy(du, p, True).wait_recv()
        for d in range(1, far):
            part = slice(d * classes, (d + 1) * classes)
            value = own[slot(0, p), part]
            for du in range(1, outer):
                value += row_recv[du - 1, p, part].astype(F32)
            core_send[0, 0, p, part] = value.astype(BF16)
            far_copy(d, p).start()

    for d in range(1, far):
        resp_far(d).wait_recv()
    resp_recv[0] = resp_send[0]
    pair = near * rows
    total = rows * n_cls
    for t in range(-(-total // LANES)):
        value = jnp.zeros((classes, LANES), F32)
        source = lane // pair + t * (LANES // pair)
        for j in range(far):
            value = jnp.where(source == lax.rem(q + j, far), resp_recv[j], value)
        width = min(LANES, total - t * LANES)
        resp_ref[:, t * LANES : t * LANES + width] = value[:, :width]

    for p in range(steps):
        for du in range(1, outer):
            row_copy(du, p, False).wait_recv()
            own[slot(0, p), :classes] += row_recv[du - 1, p, :classes].astype(F32)

    for d in range(1, n_img):
        mass_img(d).wait_recv()
    mass = mass_all[0]
    for d in range(1, n_img):
        mass += mass_all[d]
    mine = pl.ds(freq_at(my_img, 0), part_freq)
    ctf = ctf_ref[:, mine]
    denom = jnp.dot(
        mass[:, :groups], ctf * ctf * nw_ref[:, mine], precision=HIGHEST,
        preferred_element_type=F32,
    ) + prior_precision
    scale = 1.0 / denom

    for d in range(1, near):
        stat_near(d).wait_send()
        marks_near(d).wait_send()
        for p in range(steps):
            w_near(d, p).wait_send()
    for d in range(1, far):
        power_far(d).wait_send()
        resp_far(d).wait_send()
        mass_far(d).wait_send()
        for p in range(steps):
            cls_far(d, p).wait_send()
            for e in range(1, n_img):
                cls_forward(d, p, e, my_img).wait_send()
    for p in range(steps):
        for du in range(outer):
            if du:
                for dv in range(1, cores):
                    core_copy(du, dv, p).wait_send()
                row_copy(du, p, False).wait_send()
                if far > 1:
                    row_copy(du, p, True).wait_send()

    for p in range(steps):
        value = own[slot(0, p), :classes]
        for d in range(1, far):
            far_copy(d, p).wait_recv()
            value += far_recv[d, p].astype(F32)
        cols = slice(p * chunk, (p + 1) * chunk)
        for part in range(2):
            avg_ref[:, part, cols] = value[:, part * chunk : (part + 1) * chunk] * scale[:, cols]

    for d in range(1, far):
        for p in range(steps):
            far_copy(d, p).wait_send()
    for d in range(1, n_img):
        mass_img(d).wait_send()


def settle_kernel(resp_from, avg_from, resp_to, avg_to):
    resp_to[...] = resp_from[...]
    avg_to[...] = avg_from[...]


def settle(resp, avg):
    vmem = pl.BlockSpec(memory_space=pltpu.VMEM)
    return pl.pallas_call(
        settle_kernel,
        out_shape=tuple(jax.ShapeDtypeStruct(x.shape, x.dtype) for x in (resp, avg)),
        in_specs=[vmem] * 2,
        out_specs=(vmem, vmem),
    )(resp, avg)


def local(n_cls, n_img, particles, classes, ctf, noise_weight, group_ids, shifts):
    rows, _, freq = particles.shape
    cls_rows = classes.shape[0]
    poses = shifts.shape[0]
    groups = ctf.shape[0]
    total = rows * n_cls
    part_freq = freq // n_img
    chunk = 384 if part_freq % 384 == 0 else LANES
    pad_groups = -(-groups // LANES) * LANES
    near = 2 if n_cls % 2 == 0 else 1
    cores = 2 if n_img % 2 == 0 else 1
    far = n_cls // near
    outer = n_img // cores
    steps = part_freq // chunk
    held = far * cls_rows
    wide = 2 * chunk
    block = poses * rows
    vmem = pl.BlockSpec(memory_space=pltpu.VMEM)
    dma = pltpu.SemaphoreType.DMA
    most = max(1, outer - 1)
    scratch = [
        ((rows, 2, freq), BF16),
        ((far, steps, n_img, cls_rows, 2, chunk), BF16),
        ((groups, freq), F32),
        ((1, freq), F32),
        ((rows, freq), F32),
        ((rows, pad_groups), F32),
        ((near, rows, pad_groups), BF16),
        ((near * block, pad_groups), BF16),
        ((poses, freq), F32),
        ((poses, freq), F32),
        ((steps, near, rows, n_img * wide), BF16),
        ((steps, near * block, n_img * wide), BF16),
        ((2 * held, n_img * chunk), BF16),
        ((2 * cls_rows, pad_groups), F32),
        ((far, cls_rows, pad_groups), F32),
        ((near * block // LANES, 2 * held, LANES), F32),
        ((held, near * block), F32),
        ((held, near * block), BF16),
        ((near, -(-2 * near // 8) * 8, LANES), F32),
        ((far, cls_rows, LANES), F32),
        ((far, cls_rows, LANES), F32),
        ((far, cls_rows, pad_groups), F32),
        ((far, cls_rows, pad_groups), F32),
        ((n_img, cls_rows, pad_groups), F32),
        ((outer, max(1, cores - 1), steps, held, wide), BF16),
        ((outer, max(1, cores - 1), steps, held, wide), BF16),
        ((most, steps, held, wide), BF16),
        ((most, steps, held, wide), BF16),
        ((far, steps, cls_rows, wide), BF16),
        ((most * steps + 1, held, wide), F32),
    ]
    sems = [(far, steps), (far, steps, n_img), (near, steps), (near,), (far,), (near,), (far,), (far,), (n_img,)]
    sems += [(outer, cores, steps), (outer, steps), (outer, steps), (far, steps)]
    resp, avg = pl.pallas_call(
        functools.partial(kernel, n_cls, n_img, near, cores, chunk),
        out_shape=(pltpu.VMEM((cls_rows, total), F32), pltpu.VMEM((cls_rows, 2, part_freq), F32)),
        in_specs=[pl.BlockSpec(memory_space=pltpu.SMEM)] * 2
        + [pl.BlockSpec(memory_space=pl.ANY)] * 4,
        out_specs=(vmem, vmem),
        scratch_shapes=[pltpu.VMEM(*s) for s in scratch]
        + [dma((3,)), dma((n_img, steps))]
        + [dma(s) for s in sems for _ in range(2)],
        compiler_params=pltpu.CompilerParams(
            collective_id=0, has_side_effects=True, vmem_limit_bytes=61 << 20
        ),
    )(
        group_ids,
        shifts.T,
        particles,
        classes,
        ctf,
        noise_weight,
    )
    resp, avg = settle(*(pltpu.with_memory_space_constraint(x, pltpu.VMEM) for x in (resp, avg)))
    return resp.T, avg


def solution(mesh):
    placed = (
        P(("groups", "img", "cls"), None, None),
        P(("groups", "cls"), None, None),
        P("groups", None),
        P("groups"),
        P(("groups", "img", "cls")),
        P("groups", None),
    )
    return jax.shard_map(
        functools.partial(local, mesh.shape["cls"], mesh.shape["img"]),
        mesh=mesh,
        in_specs=placed,
        out_specs=(P(("groups", "img"), "cls"), P(("groups", "cls"), None, "img")),
        check_vma=False,
    )
```
